512 devices in a mesh: leaf: 64 (over x, z), front: 8 (over y, core).
Axes of the slice: x: 4, y: 4, z: 16, core: 2. Of those that a mesh axis runs over, the one named last changes fastest.
Arguments:
- interior_disp: float32 [64, 98304], P(None, 'leaf'), may hold values from -6 to 6
- separator_disp: float32 [64, 3072], P(None, 'leaf'), may hold values from -6 to 6
- modulus: float32 [64, 524288], P(None, ('leaf', 'front')), may hold values from 0.05 to 0.5
- connectivity: int32 [8, 524288], P(None, ('leaf', 'front')), may hold values from 0 to 543
- stiffness: float32 [24, 24], replicated, may hold values from -1.25 to 1.25
- load: float32 [64, 98304], P(None, ('leaf', 'front')), may hold values from -6 to 6
- leaf_pivot_inv: bfloat16 [98304, 1536], P(('leaf', 'front')), may hold values from -0.15625 to 0.15625
- leaf_coupling: bfloat16 [98304, 96], P(('leaf', 'front')), may hold values from -0.109375 to 0.109375
- pivot_inv: bfloat16 [3072, 6048], P('leaf'), may hold values from -2 to 2
- coupling: bfloat16 [3072, 5952], P('leaf'), may hold values from -2 to 2
Outputs:
- leaf_correction: float32 [64, 98304], P(None, ('leaf', 'front'))
- separator_correction: float32 [64, 18432], P('front', 'leaf')
The draws below stay inside these ranges and needn't reach their ends.
Inputs may be any that keep to these rules, and one draw needn't show every extreme that they name: `connectivity`: local node numbers below 512 are nodes inside the element's leaf subtree; number 512 + n is node n of the separator between the element's leaf and its sibling.
All inputs are finite; a program needn't handle non-finite values.
Results may differ from the reference program's by a relative error of at most 0.019.
Values may be sent and summed in bfloat16 or wider, within the bound.
No kernel may reach another device: no remote copies, remote signals or barrier semaphores. Data moves between devices by JAX's collectives and lax.ppermute only.
A program may use at most 128 MiB of HBM per device.

```python
import math
import jax
import jax.numpy as jnp
import numpy as np
from jax import lax

SAMPLES = 64
NL = 1536
ROWS = 48
LEAVES = 64
LEVELS = 6
LEAF_NODES = 512
SEP_NODES = 32
ELEMS = 524288
ZCOLS = 6048
WCOLS = 5952


def band_scales(first_level, last_level):
    return np.concatenate([np.full((ROWS * 2 ** height,), (ROWS * 2 ** height) ** (-0.5), np.float32) for height in range(first_level, last_level + 1)])


def draw_packed(key, columns, scales):
    entries = jnp.clip(jax.random.normal(key, (LEAVES * ROWS, columns), jnp.float32), -4.0, 4.0)
    return (entries * jnp.asarray(scales)[None, :]).astype(jnp.bfloat16)


def draw_pivot_inv(key, part):
    return draw_packed(jax.random.fold_in(key, 11), ZCOLS, band_scales(1, LEVELS))


def draw_coupling(key, part):
    return draw_packed(jax.random.fold_in(key, 23), WCOLS, band_scales(2, LEVELS))


def place_ends(result, own_key, low, largest):
    extent = result.shape
    spot = [jax.random.randint(jax.random.fold_in(own_key, axis), (), 0, extent[axis]) for axis in range(len(extent))]
    result = result.at[tuple(spot)].set(low)
    longest = extent.index(max(extent))
    spot[longest] = (spot[longest] + 1) % extent[longest]
    return result.at[tuple(spot)].set(largest)


def steps_of(key, shape, split, smallest, high):
    level = 1.0
    for axis_at, parts in split:
        heights = jax.random.uniform(jax.random.fold_in(jax.random.fold_in(key, 6), axis_at), (parts,), jnp.float32, smallest / len(split), high / len(split))
        level = level * jnp.repeat(jnp.exp(heights), shape[axis_at] // parts).reshape((-1,) + (1,) * (len(shape) - 1 - axis_at))
    return level


def normal_values(own_key, extent, width, bound, pieces=(), kind=jnp.bfloat16):
    loudness = steps_of(own_key, extent, pieces, -0.22, 0.18) if pieces else 1.0
    drawn = jax.random.normal(own_key, extent, jnp.float32) * width * loudness
    return jnp.minimum(jnp.maximum(drawn, -bound), bound).astype(kind)


def setup_inputs(seed: int = 0) -> dict:
    key_of = jax.random.split(jax.random.key(seed), 11)
    interior_disp = normal_values(key_of[0], (SAMPLES, LEAVES * NL), 1.0, 6.0, ((1, 64),), jnp.float32)
    separator_disp = normal_values(key_of[1], (SAMPLES, LEAVES * ROWS), 1.0, 6.0, ((1, 64),), jnp.float32)
    modulus = jnp.clip(jnp.exp(math.log(0.5) - 2.3025851 * jax.random.uniform(key_of[2], (SAMPLES, ELEMS), jnp.float32) ** steps_of(key_of[2], (SAMPLES, ELEMS), ((1, 512),), -0.2, 0.2)), 0.05, 0.5)
    connectivity = place_ends(jax.random.randint(key_of[3], (8, ELEMS), 0, LEAF_NODES + SEP_NODES), jax.random.fold_in(key_of[3], 1), 0, (LEAF_NODES + SEP_NODES) - 1).astype(jnp.int32)
    stiffness = normal_values(key_of[4], (24, 24), 24 ** -0.5, 1.25, (), jnp.float32)
    load = normal_values(key_of[5], (SAMPLES, LEAVES * NL), 1.0, 6.0, ((1, 512),), jnp.float32)
    leaf_pivot_inv = normal_values(key_of[6], (LEAVES * NL, NL), NL ** -0.5, 0.15625, ((0, 512),))
    leaf_coupling = normal_values(key_of[7], (LEAVES * NL, 2 * ROWS), (2 * NL) ** -0.5, 0.109375, ((0, 512),))
    pivot_inv = draw_pivot_inv(jax.random.fold_in(key_of[10], 71), 0)
    coupling = draw_coupling(jax.random.fold_in(key_of[10], 71), 0)
    return dict(interior_disp=interior_disp, separator_disp=separator_disp, modulus=modulus, connectivity=connectivity, stiffness=stiffness, load=load, leaf_pivot_inv=leaf_pivot_inv, leaf_coupling=leaf_coupling, pivot_inv=pivot_inv, coupling=coupling)


def rounded(value):
    return lax.optimization_barrier(value.astype(jnp.bfloat16)).astype(jnp.float32)


def reference(interior_disp, separator_disp, modulus, connectivity, stiffness, load, leaf_pivot_inv, leaf_coupling, pivot_inv, coupling):
    highest = lax.Precision.HIGHEST
    per_leaf = ELEMS // LEAVES
    table_size = NL + 2 * ROWS

    def leaf_work(leaf_number):
        inner_part = lax.dynamic_slice_in_dim(interior_disp, leaf_number * NL, NL, 1)
        shared_part = lax.dynamic_slice_in_dim(separator_disp, (leaf_number // 2) * (2 * ROWS), 2 * ROWS, 1)
        node_rows = jnp.concatenate([inner_part, shared_part], 1).T
        corner_nodes = lax.dynamic_slice_in_dim(connectivity, leaf_number * per_leaf, per_leaf, 1)
        moduli = lax.dynamic_slice_in_dim(modulus, leaf_number * per_leaf, per_leaf, 1)
        dof_slots = (3 * corner_nodes[:, None, :] + jnp.arange(3, dtype=jnp.int32)[None, :, None]).reshape(24, per_leaf)
        corners = jnp.take(node_rows, dof_slots, axis=0)
        forces = jnp.einsum("ij,jes->ies", stiffness, corners, precision=highest) * moduli.T[None, :, :]
        assembled = jax.ops.segment_sum(forces.reshape(24 * per_leaf, SAMPLES), dof_slots.reshape(-1), num_segments=table_size).T
        residual = lax.dynamic_slice_in_dim(load, leaf_number * NL, NL, 1) - assembled[:, :NL]
        low_residual = residual.astype(jnp.bfloat16)
        pivot_rows = lax.dynamic_slice_in_dim(leaf_pivot_inv, leaf_number * NL, NL, 0)
        pivoted = residual + jnp.dot(low_residual, pivot_rows.T, preferred_element_type=jnp.float32)
        leaf_rows = lax.dynamic_slice_in_dim(leaf_coupling, leaf_number * NL, NL, 0)
        terms = -assembled[:, NL:] - jnp.dot(low_residual, leaf_rows, preferred_element_type=jnp.float32)
        return pivoted, terms

    pivoted_all, sep_terms = lax.map(leaf_work, jnp.arange(LEAVES, dtype=jnp.int32))
    pairs = LEAVES // 2
    level_rhs = sep_terms.reshape(pairs, 2, SAMPLES, 2 * ROWS).sum(1)
    level_rhs = jnp.transpose(level_rhs, (1, 0, 2)).reshape(SAMPLES, LEAVES * ROWS)
    pivoted_levels = []
    for height in range(1, LEVELS + 1):
        front_count = LEAVES >> height
        front_size = ROWS << height
        if height > 1:
            band_start = ROWS * (2 ** height - 4)
            coupling_band = coupling[:, band_start:band_start + front_size].reshape(front_count, front_size, front_size).astype(jnp.float32)
            children = rounded(level_rhs.reshape(SAMPLES, front_count, front_size))
            level_rhs = -jnp.einsum("sjc,jcp->sjp", children, coupling_band, precision=highest).reshape(SAMPLES, LEAVES * ROWS)
        band_start = ROWS * (2 ** height - 2)
        pivot_band = pivot_inv[:, band_start:band_start + front_size].reshape(front_count, front_size, front_size).astype(jnp.float32)
        fronts_low = rounded(level_rhs.reshape(SAMPLES, front_count, front_size))
        pivoted_levels.append(level_rhs + jnp.einsum("sjc,jrc->sjr", fronts_low, pivot_band, precision=highest).reshape(SAMPLES, LEAVES * ROWS))
    solved_levels = [None] * LEVELS
    current = pivoted_levels[LEVELS - 1]
    for height in range(LEVELS, 0, -1):
        solved_levels[height - 1] = current
        if height > 1:
            front_count = LEAVES >> height
            front_size = ROWS << height
            band_start = ROWS * (2 ** height - 4)
            coupling_band = coupling[:, band_start:band_start + front_size].reshape(front_count, front_size, front_size).astype(jnp.float32)
            parent_low = rounded(current.reshape(SAMPLES, front_count, front_size))
            current = pivoted_levels[height - 2] - jnp.einsum("sjp,jcp->sjc", parent_low, coupling_band, precision=highest).reshape(SAMPLES, LEAVES * ROWS)
    leaf_pivoted = jnp.transpose(pivoted_all, (1, 0, 2)).reshape(SAMPLES, pairs, 2 * NL)
    leaf_band = leaf_coupling.reshape(pairs, 2 * NL, 2 * ROWS).astype(jnp.float32)
    parent_low = rounded(current.reshape(SAMPLES, pairs, 2 * ROWS))
    leaf_correction = (leaf_pivoted - jnp.einsum("sjp,jcp->sjc", parent_low, leaf_band, precision=highest)).reshape(SAMPLES, LEAVES * NL)
    separator_correction = jnp.stack([value.reshape(SAMPLES, LEAVES, ROWS) for value in solved_levels], axis=2).reshape(SAMPLES, LEAVES * LEVELS * ROWS)
    return leaf_correction, separator_correction
```

```python
import jax
import jax.numpy as jnp
from jax import lax
from jax.experimental import pallas as pl
from jax.experimental.pallas import tpu as pltpu
from jax.sharding import PartitionSpec as P

BF = jnp.bfloat16
F32 = jnp.float32
ROW_CONTRACT = (((1,), (1,)), ((), ()))
TILE = 256


def rows_dot(left, right):
    return lax.dot_general(left, right, ROW_CONTRACT, preferred_element_type=F32)


def plain_dot(left, right):
    return jnp.dot(left, right, preferred_element_type=F32)


def iota(shape, dim):
    return lax.broadcasted_iota(jnp.int32, shape, dim)


def spread(components, nodes):
    size = components * nodes
    column = iota((size, size), 1)
    comp = sum((column >= nodes * k).astype(jnp.int32) for k in range(1, components))
    return jnp.where(iota((size, size), 0) == components * (column - comp * nodes) + comp, 1.0, 0.0).astype(BF)


def element_kernel(disp_ref, shared_ref, modulus_ref, conn_ref, stiff_ref, pieces_ref, sep_ref,
                   table_ref, onehot_ref, kron_ref, gather_ref, force_ref, acc_ref):
    samples, inner = disp_ref.shape
    shared = shared_ref.shape[1]
    elements = conn_ref.shape[1]
    nodes = inner // 3
    sep_nodes = shared // 3
    all_nodes = nodes + sep_nodes
    blocks = samples // 8
    sort = spread(3, 128)
    for chunk in range(nodes // 128):
        part = plain_dot(disp_ref[:, chunk * 384:(chunk + 1) * 384].astype(BF), sort)
        for block in range(blocks):
            for comp in range(3):
                row = block * 24 + comp * 8
                table_ref[row:row + 8, chunk * 128:(chunk + 1) * 128] = part[
                    block * 8:block * 8 + 8, comp * 128:(comp + 1) * 128]
    column = iota((shared, 384), 1)
    comp_of = (column >= 128).astype(jnp.int32) + (column >= 256).astype(jnp.int32)
    local = column - 128 * comp_of
    sep_sort = jnp.where((iota((shared, 384), 0) == 3 * local + comp_of) & (local < sep_nodes), 1.0, 0.0).astype(BF)
    part = plain_dot(shared_ref[...].astype(BF), sep_sort)
    for block in range(blocks):
        for comp in range(3):
            row = block * 24 + comp * 8
            table_ref[row:row + 8, nodes:nodes + 128] = part[
                block * 8:block * 8 + 8, comp * 128:(comp + 1) * 128]
    table = table_ref[:, :all_nodes].astype(BF)
    up = jnp.where((iota((192, 24), 0) >> 3) == iota((192, 24), 1), 1.0, 0.0).astype(BF)
    wide = rows_dot(plain_dot(up, stiff_ref[...].astype(BF)).astype(BF), up)
    same = (iota((192, 192), 0) & 7) == (iota((192, 192), 1) & 7)
    kron_ref[...] = jnp.where(same, wide, 0.0).astype(BF)
    acc_ref[...] = jnp.zeros_like(acc_ref)

    def tile_step(tile, carry):
        start = pl.multiple_of(tile * TILE, TILE)
        node_row = iota((all_nodes, TILE), 0)
        for corner in range(8):
            which = conn_ref[corner:corner + 1, pl.ds(start, TILE)]
            onehot_ref[:, corner * TILE:(corner + 1) * TILE] = jnp.where(
                node_row == which, 1.0, 0.0).astype(BF)
        for corner in range(8):
            gather_ref[:, corner * TILE:(corner + 1) * TILE] = plain_dot(
                table, onehot_ref[:, corner * TILE:(corner + 1) * TILE])
        for block in range(blocks):
            corners = jnp.concatenate(
                [gather_ref[block * 24:block * 24 + 24, corner * TILE:(corner + 1) * TILE] for corner in range(8)],
                0).astype(BF)
            forces = plain_dot(kron_ref[...], corners)
            scale = modulus_ref[block * 8:block * 8 + 8, pl.ds(start, TILE)]
            forces = forces.reshape(24, 8, TILE) * scale[None]
            forces = forces.reshape(192, TILE)
            for corner in range(8):
                force_ref[block * 24:block * 24 + 24, corner * TILE:(corner + 1) * TILE] = forces[
                    corner * 24:corner * 24 + 24]
        acc_ref[...] += rows_dot(force_ref[...].astype(BF), onehot_ref[...])
        return carry

    lax.fori_loop(0, elements // TILE, tile_step, 0)

    def by_component(first, width):
        rows = []
        for comp in range(3):
            rows.append(jnp.concatenate(
                [acc_ref[block * 24 + comp * 8:block * 24 + comp * 8 + 8, first:first + width]
                 for block in range(blocks)], 0))
        return jnp.concatenate(rows, 1)

    for chunk in range(nodes // 128):
        low = by_component(chunk * 128, 128).astype(BF)
        back = rows_dot(low, sort).astype(BF)
        pieces_ref[2 * chunk] = back[:, :192]
        pieces_ref[2 * chunk + 1] = back[:, 192:]
    rows = []
    for comp in range(3):
        rows.append(jnp.concatenate(
            [acc_ref[block * 24 + comp * 8:block * 24 + comp * 8 + 8, nodes:all_nodes] for block in range(blocks)], 0))
    total = jnp.zeros((samples, shared), F32)
    for comp in range(3):
        place = jnp.where(iota((sep_nodes, shared), 1) == 3 * iota((sep_nodes, shared), 0) + comp, 1.0, 0.0).astype(BF)
        high = rows[comp].astype(BF)
        rest = (rows[comp] - high.astype(F32)).astype(BF)
        total = total + plain_dot(high, place) + plain_dot(rest, place)
    sep_ref[...] = total


def assemble(disp, shared, modulus, connectivity, stiffness, pieces):
    samples, inner = disp.shape
    all_nodes = (inner + shared.shape[1]) // 3
    padded = inner // 3 + 128
    return pl.pallas_call(
        element_kernel,
        out_shape=(
            jax.ShapeDtypeStruct((pieces, samples, inner // pieces), BF),
            jax.ShapeDtypeStruct((samples, shared.shape[1]), F32),
        ),
        scratch_shapes=[
            pltpu.VMEM((3 * samples, padded), F32),
            pltpu.VMEM((all_nodes, 8 * TILE), BF),
            pltpu.VMEM((192, 192), BF),
            pltpu.VMEM((3 * samples, 8 * TILE), F32),
            pltpu.VMEM((3 * samples, 8 * TILE), F32),
            pltpu.VMEM((3 * samples, all_nodes), F32),
        ],
        compiler_params=pltpu.CompilerParams(vmem_limit_bytes=40 << 20),
        name="elements",
    )(disp, shared, modulus, connectivity, stiffness)


def exchange(value, axis, groups=None):
    return lax.all_to_all(value, axis, 0, 0, axis_index_groups=groups, tiled=True)


def group_lists(leaves, height):
    size = 1 << height
    return [[base + i for i in range(size)] for base in range(0, leaves, size)]


def body(
    interior_disp,
    separator_disp,
    modulus,
    connectivity,
    stiffness,
    load,
    leaf_pivot_inv,
    leaf_coupling,
    pivot_inv,
    coupling,
):
    leaves = lax.axis_size("leaf")
    fronts = lax.axis_size("front")
    levels = leaves.bit_length() - 1
    leaf_index = lax.axis_index("leaf")
    samples, inner_size = interior_disp.shape
    rows = separator_disp.shape[1]
    own_samples = samples // fronts
    pairs = [(source, source ^ 1) for source in range(leaves)]
    partner = lax.ppermute(separator_disp, "leaf", pairs)
    upper_leaf = leaf_index % 2 == 1
    shared = jnp.where(
        upper_leaf,
        jnp.concatenate([partner, separator_disp], 1),
        jnp.concatenate([separator_disp, partner], 1),
    )
    pieces, sep_terms = assemble(interior_disp, shared, modulus, connectivity, stiffness, fronts)
    received = exchange(pieces, "front")
    own_residual = load - jnp.sum(received.astype(F32), 0)
    own_low = own_residual.astype(BF)
    terms = -sep_terms - plain_dot(own_low, leaf_coupling)
    parts = exchange(terms.reshape(fronts, own_samples, 2 * rows), "front")
    term = jnp.sum(parts, 0)
    everyone = exchange(jnp.broadcast_to(own_low[None], (fronts,) + own_low.shape), "front")
    low_residual = jnp.transpose(everyone, (1, 0, 2)).reshape(samples, inner_size)
    pivoted = own_residual + rows_dot(low_residual, leaf_pivot_inv)

    level_part = term
    fulls = []
    own_pieces = []
    for height in range(1, levels + 1):
        size = 1 << height
        front_size = rows << height
        if height > 1:
            band = rows * (2**height - 4)
            level_part = -plain_dot(own_pieces[-1].astype(BF), coupling[:, band:band + front_size])
        outgoing = jnp.transpose(level_part.astype(BF).reshape(own_samples, size, rows), (1, 0, 2))
        incoming = exchange(outgoing, "leaf", group_lists(leaves, height))
        own_pieces.append(jnp.sum(incoming.astype(F32), 0))

    def collect(low, height):
        size = 1 << height
        sent = jnp.broadcast_to(low[None], (size,) + low.shape)
        return exchange(sent, "leaf", group_lists(leaves, height))

    low_pieces = jnp.concatenate([piece.astype(BF) for piece in own_pieces], 1)
    gathered = collect(low_pieces, levels)
    pivot_parts = []
    for height in range(1, levels + 1):
        size = 1 << height
        front_size = rows << height
        band = rows * (2**height - 2)
        base = leaf_index // size * size
        mine = lax.dynamic_slice_in_dim(gathered, base, size, 0)[:, :, (height - 1) * rows:height * rows]
        full = jnp.transpose(mine, (1, 0, 2)).reshape(own_samples, front_size)
        pivot_parts.append(own_pieces[height - 1] + rows_dot(full, pivot_inv[:, band:band + front_size]))
    corrections = [None] * levels
    current = pivot_parts[levels - 1]
    for height in range(levels, 0, -1):
        corrections[height - 1] = current
        front_size = rows << height
        incoming = collect(current.astype(BF), height)
        front_low = jnp.transpose(incoming, (1, 0, 2)).reshape(own_samples, front_size)
        if height > 1:
            band = rows * (2**height - 4)
            current = pivot_parts[height - 2] - rows_dot(front_low, coupling[:, band:band + front_size])
    all_samples = exchange(jnp.broadcast_to(front_low[None], (fronts,) + front_low.shape), "front")
    leaf_correction = pivoted - rows_dot(all_samples.reshape(samples, 2 * rows), leaf_coupling)
    return (leaf_correction, jnp.concatenate(corrections, 1))


def solution(mesh):
    in_specs = (
        P(None, "leaf"),
        P(None, "leaf"),
        P(None, ("leaf", "front")),
        P(None, ("leaf", "front")),
        P(),
        P(None, ("leaf", "front")),
        P(("leaf", "front"), None),
        P(("leaf", "front"), None),
        P("leaf", None),
        P("leaf", None),
    )
    out_specs = (P(None, ("leaf", "front")), P("front", "leaf"))
    return jax.shard_map(body, mesh=mesh, in_specs=in_specs, out_specs=out_specs, check_vma=False)
```

```python
import jax
import jax.numpy as jnp
from jax import lax
from jax.experimental import pallas as pl
from jax.experimental.pallas import tpu as pltpu
from jax.sharding import PartitionSpec as P

BF = jnp.bfloat16
F32 = jnp.float32
ROW_CONTRACT = (((1,), (1,)), ((), ()))
TILE = 256


def rows_dot(left, right):
    return lax.dot_general(left, right, ROW_CONTRACT, preferred_element_type=F32)


def plain_dot(left, right):
    return jnp.dot(left, right, preferred_element_type=F32)


def iota(shape, dim):
    return lax.broadcasted_iota(jnp.int32, shape, dim)


def spread(components, nodes):
    size = components * nodes
    column = iota((size, size), 1)
    comp = sum((column >= nodes * k).astype(jnp.int32) for k in range(1, components))
    return jnp.where(iota((size, size), 0) == components * (column - comp * nodes) + comp, 1.0, 0.0).astype(BF)


def element_kernel(disp_ref, shared_ref, modulus_ref, conn_ref, stiff_ref, pieces_ref, sep_ref,
                   table_ref, onehot_ref, kron_ref, gather_ref, force_ref, acc_ref):
    samples, inner = disp_ref.shape
    shared = shared_ref.shape[1]
    elements = conn_ref.shape[1]
    nodes = inner // 3
    sep_nodes = shared // 3
    all_nodes = nodes + sep_nodes
    blocks = samples // 8
    sort = spread(3, 128)
    for chunk in range(nodes // 128):
        part = plain_dot(disp_ref[:, chunk * 384:(chunk + 1) * 384].astype(BF), sort)
        for block in range(blocks):
            for comp in range(3):
                row = block * 24 + comp * 8
                table_ref[row:row + 8, chunk * 128:(chunk + 1) * 128] = part[
                    block * 8:block * 8 + 8, comp * 128:(comp + 1) * 128]
    column = iota((shared, 384), 1)
    comp_of = (column >= 128).astype(jnp.int32) + (column >= 256).astype(jnp.int32)
    local = column - 128 * comp_of
    sep_sort = jnp.where((iota((shared, 384), 0) == 3 * local + comp_of) & (local < sep_nodes), 1.0, 0.0).astype(BF)
    part = plain_dot(shared_ref[...].astype(BF), sep_sort)
    for block in range(blocks):
        for comp in range(3):
            row = block * 24 + comp * 8
            table_ref[row:row + 8, nodes:nodes + 128] = part[
                block * 8:block * 8 + 8, comp * 128:(comp + 1) * 128]
    table = table_ref[:, :all_nodes].astype(BF)
    up = jnp.where((iota((192, 24), 0) >> 3) == iota((192, 24), 1), 1.0, 0.0).astype(BF)
    wide = rows_dot(plain_dot(up, stiff_ref[...].astype(BF)).astype(BF), up)
    same = (iota((192, 192), 0) & 7) == (iota((192, 192), 1) & 7)
    kron_ref[...] = jnp.where(same, wide, 0.0).astype(BF)
    acc_ref[...] = jnp.zeros_like(acc_ref)

    def tile_step(tile, carry):
        start = pl.multiple_of(tile * TILE, TILE)
        node_row = iota((all_nodes, TILE), 0)
        for corner in range(8):
            which = conn_ref[corner:corner + 1, pl.ds(start, TILE)]
            onehot_ref[:, corner * TILE:(corner + 1) * TILE] = jnp.where(
                node_row == which, 1.0, 0.0).astype(BF)
        for corner in range(8):
            gather_ref[:, corner * TILE:(corner + 1) * TILE] = plain_dot(
                table, onehot_ref[:, corner * TILE:(corner + 1) * TILE])
        for block in range(blocks):
            corners = jnp.concatenate(
                [gather_ref[block * 24:block * 24 + 24, corner * TILE:(corner + 1) * TILE] for corner in range(8)],
                0).astype(BF)
            forces = plain_dot(kron_ref[...], corners)
            scale = modulus_ref[block * 8:block * 8 + 8, pl.ds(start, TILE)]
            forces = forces.reshape(24, 8, TILE) * scale[None]
            forces = forces.reshape(192, TILE)
            for corner in range(8):
                force_ref[block * 24:block * 24 + 24, corner * TILE:(corner + 1) * TILE] = forces[
                    corner * 24:corner * 24 + 24]
        acc_ref[...] += rows_dot(force_ref[...].astype(BF), onehot_ref[...])
        return carry

    lax.fori_loop(0, elements // TILE, tile_step, 0)

    def by_component(first, width):
        rows = []
        for comp in range(3):
            rows.append(jnp.concatenate(
                [acc_ref[block * 24 + comp * 8:block * 24 + comp * 8 + 8, first:first + width]
                 for block in range(blocks)], 0))
        return jnp.concatenate(rows, 1)

    for chunk in range(nodes // 128):
        low = by_component(chunk * 128, 128).astype(BF)
        back = rows_dot(low, sort).astype(BF)
        pieces_ref[2 * chunk] = back[:, :192]
        pieces_ref[2 * chunk + 1] = back[:, 192:]
    rows = []
    for comp in range(3):
        rows.append(jnp.concatenate(
            [acc_ref[block * 24 + comp * 8:block * 24 + comp * 8 + 8, nodes:all_nodes] for block in range(blocks)], 0))
    total = jnp.zeros((samples, shared), F32)
    for comp in range(3):
        place = jnp.where(iota((sep_nodes, shared), 1) == 3 * iota((sep_nodes, shared), 0) + comp, 1.0, 0.0).astype(BF)
        high = rows[comp].astype(BF)
        rest = (rows[comp] - high.astype(F32)).astype(BF)
        total = total + plain_dot(high, place) + plain_dot(rest, place)
    sep_ref[...] = total


def assemble(disp, shared, modulus, connectivity, stiffness, pieces):
    samples, inner = disp.shape
    all_nodes = (inner + shared.shape[1]) // 3
    padded = inner // 3 + 128
    return pl.pallas_call(
        element_kernel,
        out_shape=(
            jax.ShapeDtypeStruct((pieces, samples, inner // pieces), BF),
            jax.ShapeDtypeStruct((samples, shared.shape[1]), F32),
        ),
        scratch_shapes=[
            pltpu.VMEM((3 * samples, padded), F32),
            pltpu.VMEM((all_nodes, 8 * TILE), BF),
            pltpu.VMEM((192, 192), BF),
            pltpu.VMEM((3 * samples, 8 * TILE), F32),
            pltpu.VMEM((3 * samples, 8 * TILE), F32),
            pltpu.VMEM((3 * samples, all_nodes), F32),
        ],
        compiler_params=pltpu.CompilerParams(vmem_limit_bytes=40 << 20),
        name="elements",
    )(disp, shared, modulus, connectivity, stiffness)


def exchange(value, axis, groups=None):
    return lax.all_to_all(value, axis, 0, 0, axis_index_groups=groups, tiled=True)


def group_lists(leaves, height):
    size = 1 << height
    return [[base + i for i in range(size)] for base in range(0, leaves, size)]


def body(
    interior_disp,
    separator_disp,
    modulus,
    connectivity,
    stiffness,
    load,
    leaf_pivot_inv,
    leaf_coupling,
    pivot_inv,
    coupling,
):
    leaves = lax.axis_size("leaf")
    fronts = lax.axis_size("front")
    levels = leaves.bit_length() - 1
    leaf_index = lax.axis_index("leaf")
    samples, inner_size = interior_disp.shape
    rows = separator_disp.shape[1]
    own_samples = samples // fronts
    pairs = [(source, source ^ 1) for source in range(leaves)]
    partner = lax.ppermute(separator_disp, "leaf", pairs)
    upper_leaf = leaf_index % 2 == 1
    shared = jnp.where(
        upper_leaf,
        jnp.concatenate([partner, separator_disp], 1),
        jnp.concatenate([separator_disp, partner], 1),
    )
    near = 8
    near_cols = -(-rows * (2**5 - 4) // 128) * 128
    near_groups = [[base + i for i in range(near)] for base in range(0, leaves, near)]
    ring_groups = group_lists(leaves, 4)
    spot = leaf_index % near
    near_bands = lax.all_gather(coupling[:, :near_cols], "leaf", axis_index_groups=near_groups)
    start5 = rows * (2**5 - 4)
    ring_band = lax.all_gather(
        lax.optimization_barrier((coupling, near_bands))[0][:, start5:2 * start5 + 4 * rows], "leaf",
        axis_index_groups=ring_groups,
    ).reshape(16 * rows, 32 * rows)

    def band(height, width):
        start = rows * (2**height - 4)
        return near_bands[:, :, start:start + width].reshape(near * rows, width)

    def own_coupling(height):
        start = rows * (2**height - 4)
        return coupling[:, start:start + (rows << height)]

    def own_pivot(height):
        start = rows * (2**height - 2)
        return pivot_inv[:, start:start + (rows << height)]

    def joined(stack):
        return jnp.transpose(stack, (1, 0, 2)).reshape(own_samples, -1)

    def split(flat):
        return jnp.transpose(flat.reshape(own_samples, -1, rows), (1, 0, 2))

    def collect(low, height):
        sent = jnp.broadcast_to(low[None], (1 << height,) + low.shape)
        return exchange(sent, "leaf", group_lists(leaves, height))

    pieces, sep_terms = assemble(interior_disp, shared, modulus, connectivity, stiffness, fronts)
    received = exchange(pieces, "front")
    own_residual = load - jnp.sum(received.astype(F32), 0)
    own_low = own_residual.astype(BF)
    terms = -sep_terms - plain_dot(own_low, leaf_coupling)
    high = lax.reduce_precision(terms, 8, 7)
    both = jnp.concatenate([high, terms - high], 1).astype(BF).reshape(fronts, own_samples, 4 * rows)
    packed = jnp.concatenate([jnp.broadcast_to(own_low[None], (fronts,) + own_low.shape), both], 1)
    everyone = exchange(packed, "front")
    halves = jnp.sum(everyone[:, samples:].astype(F32), 0)
    term = halves[:, :2 * rows] + halves[:, 2 * rows:]
    low_residual = jnp.transpose(everyone[:, :samples], (1, 0, 2)).reshape(samples, inner_size)
    pivoted = own_residual + rows_dot(low_residual, leaf_pivot_inv)

    near_terms = exchange(jnp.broadcast_to(term.astype(BF)[None], (near,) + term.shape), "leaf", near_groups)
    paired = near_terms.reshape(near // 2, 2, own_samples, 2 * rows).astype(F32).sum(1)
    q1 = jnp.transpose(paired, (1, 0, 2)).reshape(own_samples, near * rows)
    half = near * rows // 2
    band2 = band(2, half)
    band3 = band(3, 2 * half)
    band4 = band(4, 4 * half)
    low1 = q1.astype(BF)
    q2 = -jnp.concatenate(
        [plain_dot(low1[:, :half], band2[:half]), plain_dot(low1[:, half:], band2[half:])], 1)
    low2 = q2.astype(BF)
    q3 = -plain_dot(low2, band3)
    low3 = q3.astype(BF)
    part4 = (-plain_dot(low3, band4)).astype(BF)
    ring = 16
    across = []
    for source in range(leaves):
        place = source % ring
        other = place + (12 if place < 4 else -12 if place >= 12 else 4 if place < 8 else -4)
        across.append((source, source - place + other))
    q4 = part4.astype(F32) + lax.ppermute(part4, "leaf", across).astype(F32)
    low4 = q4.astype(BF)

    def piece(flat, index):
        return lax.dynamic_slice_in_dim(flat, index * rows, rows, 1)

    z_own = []
    for height, (value, low) in enumerate(((q1, low1), (q2, low2), (q3, low3)), 1):
        size = 1 << height
        front = lax.dynamic_slice_in_dim(low, spot // size * (size * rows), size * rows, 1)
        z_own.append(piece(value, spot) + rows_dot(front, own_pivot(height)))
    ring_spot = leaf_index % ring
    z4 = piece(q4, ring_spot) + rows_dot(low4, own_pivot(4))
    part5 = -plain_dot(piece(low4, ring_spot), own_coupling(5))
    q5 = jnp.sum(exchange(split(part5.astype(BF)), "leaf", group_lists(leaves, 5)).astype(F32), 0)
    low5 = q5.astype(BF)
    part6 = -plain_dot(low5, own_coupling(6))
    sent = jnp.concatenate(
        [split(part6.astype(BF)), jnp.broadcast_to(low5[None], (leaves,) + low5.shape)], 2)
    back = exchange(sent, "leaf")
    q6 = jnp.sum(back[:, :, :rows].astype(F32), 0)
    full5 = joined(lax.dynamic_slice_in_dim(back, leaf_index // 32 * 32, 32, 0)[:, :, rows:])
    z5 = q5 + rows_dot(full5, own_pivot(5))
    x6 = q6 + rows_dot(joined(collect(q6.astype(BF), 6)), own_pivot(6))
    x5 = z5 - rows_dot(joined(collect(x6.astype(BF), 6)), own_coupling(6))
    last = collect(jnp.concatenate([x5, z4] + z_own, 1).astype(BF), 5)
    same_ring = lax.dynamic_slice_in_dim(last, leaf_index % 32 // 16 * 16, 16, 0)
    x4_full = joined(same_ring[:, :, rows:2 * rows]).astype(F32) - rows_dot(joined(last[:, :, :rows]), ring_band)
    full4 = x4_full.astype(BF)
    x4 = piece(x4_full, ring_spot)
    nearby = lax.dynamic_slice_in_dim(last, leaf_index % 32 // near * near, near, 0)[:, :, rows:]
    z1, z2, z3 = (joined(nearby[:, :, rows * k:rows * (k + 1)]).astype(F32) for k in (1, 2, 3))
    x3 = z3 - rows_dot(full4, band4)
    x2 = z2 - rows_dot(x3.astype(BF), band3)
    low_x2 = x2.astype(BF)
    x1 = z1 - jnp.concatenate(
        [rows_dot(low_x2[:, :half], band2[:half]), rows_dot(low_x2[:, half:], band2[half:])], 1)
    corrections = [piece(x1, spot), piece(x2, spot), piece(x3, spot), x4, x5, x6]
    front_low = lax.dynamic_slice_in_dim(x1.astype(BF), spot // 2 * (2 * rows), 2 * rows, 1)
    all_samples = exchange(jnp.broadcast_to(front_low[None], (fronts,) + front_low.shape), "front")
    leaf_correction = pivoted - rows_dot(all_samples.reshape(samples, 2 * rows), leaf_coupling)
    return (leaf_correction, jnp.concatenate(corrections, 1))


def solution(mesh):
    in_specs = (
        P(None, "leaf"),
        P(None, "leaf"),
        P(None, ("leaf", "front")),
        P(None, ("leaf", "front")),
        P(),
        P(None, ("leaf", "front")),
        P(("leaf", "front"), None),
        P(("leaf", "front"), None),
        P("leaf", None),
        P("leaf", None),
    )
    out_specs = (P(None, ("leaf", "front")), P("front", "leaf"))
    return jax.shard_map(body, mesh=mesh, in_specs=in_specs, out_specs=out_specs, check_vma=False)
```

```python
import jax
import jax.numpy as jnp
from jax import lax
from jax.experimental import pallas as pl
from jax.experimental.pallas import tpu as pltpu
from jax.sharding import PartitionSpec as P

BF = jnp.bfloat16
F32 = jnp.float32
ROW_CONTRACT = (((1,), (1,)), ((), ()))
TILE = 1024


def rows_dot(left, right):
    return lax.dot_general(left, right, ROW_CONTRACT, preferred_element_type=F32)


def plain_dot(left, right):
    return jnp.dot(left, right, preferred_element_type=F32)


def iota(shape, dim):
    return lax.broadcasted_iota(jnp.int32, shape, dim)


def spread(components, nodes):
    size = components * nodes
    column = iota((size, size), 1)
    comp = sum((column >= nodes * k).astype(jnp.int32) for k in range(1, components))
    return jnp.where(iota((size, size), 0) == components * (column - comp * nodes) + comp, 1.0, 0.0).astype(BF)


def fetch(source, target, semaphore):
    copy = pltpu.make_async_copy(source, target, semaphore)
    copy.start()
    return copy


def prepare_kernel(disp_hbm, stiff_hbm, table_ref, kron_ref, disp_ref, stiff_ref, disp_sem, stiff_sem):
    disp_copy = fetch(disp_hbm, disp_ref, disp_sem)
    stiff_copy = fetch(stiff_hbm, stiff_ref, stiff_sem)
    samples, inner = disp_ref.shape
    blocks = samples // 8
    sort = spread(3, 128)
    up = jnp.where((iota((192, 24), 0) >> 3) == iota((192, 24), 1), 1.0, 0.0).astype(BF)
    same = (iota((192, 192), 0) & 7) == (iota((192, 192), 1) & 7)
    stiff_copy.wait()
    wide = rows_dot(plain_dot(up, stiff_ref[...].astype(BF)).astype(BF), up)
    kron_ref[...] = jnp.where(same, wide, 0.0).astype(BF)
    disp_copy.wait()
    for chunk in range(inner // 384):
        part = plain_dot(disp_ref[:, chunk * 384:(chunk + 1) * 384].astype(BF), sort)
        rows = [
            part[block * 8:block * 8 + 8, comp * 128:(comp + 1) * 128]
            for block in range(blocks) for comp in range(3)
        ]
        table_ref[:, chunk * 128:(chunk + 1) * 128] = jnp.concatenate(rows, 0).astype(BF)


def prepare(disp, stiffness):
    samples, inner = disp.shape
    return pl.pallas_call(
        prepare_kernel,
        in_specs=[pl.BlockSpec(memory_space=pl.ANY), pl.BlockSpec(memory_space=pl.ANY)],
        out_shape=(
            jax.ShapeDtypeStruct((3 * samples, inner // 3), BF),
            jax.ShapeDtypeStruct((192, 192), BF),
        ),
        scratch_shapes=[
            pltpu.VMEM(disp.shape, F32),
            pltpu.VMEM(stiffness.shape, F32),
            pltpu.SemaphoreType.DMA,
            pltpu.SemaphoreType.DMA,
        ],
        compiler_params=pltpu.CompilerParams(vmem_limit_bytes=16 << 20),
        name="prepare",
    )(disp, stiffness)


def element_kernel(shared_ref, modulus_hbm, conn_hbm, inner_table_ref, kron_ref, pieces_ref, sep_ref,
                   modulus_ref, conn_ref, table_ref, onehot_ref, gather_ref, force_ref, acc_ref,
                   modulus_sem, conn_sem):
    conn_copy = fetch(conn_hbm, conn_ref, conn_sem)
    modulus_copy = fetch(modulus_hbm, modulus_ref, modulus_sem)
    samples, shared = shared_ref.shape
    elements = conn_ref.shape[1]
    nodes = inner_table_ref.shape[1]
    sep_nodes = shared // 3
    all_nodes = nodes + sep_nodes
    blocks = samples // 8
    sort = spread(3, 128)
    table_ref[:, :nodes] = inner_table_ref[...]
    column = iota((shared, 384), 1)
    comp_of = (column >= 128).astype(jnp.int32) + (column >= 256).astype(jnp.int32)
    local = column - 128 * comp_of
    sep_sort = jnp.where((iota((shared, 384), 0) == 3 * local + comp_of) & (local < sep_nodes), 1.0, 0.0).astype(BF)
    part = plain_dot(shared_ref[...].astype(BF), sep_sort)
    rows = [
        part[block * 8:block * 8 + 8, comp * 128:(comp + 1) * 128] for block in range(blocks) for comp in range(3)
    ]
    table_ref[:, nodes:] = jnp.concatenate(rows, 0).astype(BF)
    table = table_ref[:, :all_nodes]
    conn_copy.wait()
    modulus_copy.wait()
    acc_ref[...] = jnp.zeros_like(acc_ref)

    def tile_step(tile, carry):
        start = pl.multiple_of(tile * TILE, TILE)
        node_row = iota((all_nodes, TILE), 0)
        for corner in range(8):
            which = conn_ref[corner:corner + 1, pl.ds(start, TILE)]
            onehot_ref[:, corner * TILE:(corner + 1) * TILE] = jnp.where(
                node_row == which, 1.0, 0.0).astype(BF)
        for corner in range(8):
            gather_ref[:, corner * TILE:(corner + 1) * TILE] = plain_dot(
                table, onehot_ref[:, corner * TILE:(corner + 1) * TILE])
        for block in range(blocks):
            corners = jnp.concatenate(
                [gather_ref[block * 24:block * 24 + 24, corner * TILE:(corner + 1) * TILE] for corner in range(8)],
                0).astype(BF)
            forces = plain_dot(kron_ref[...], corners)
            scale = modulus_ref[block * 8:block * 8 + 8, pl.ds(start, TILE)]
            forces = forces.reshape(24, 8, TILE) * scale[None]
            forces = forces.reshape(192, TILE)
            for corner in range(8):
                force_ref[block * 24:block * 24 + 24, corner * TILE:(corner + 1) * TILE] = forces[
                    corner * 24:corner * 24 + 24]
        acc_ref[...] += rows_dot(force_ref[...].astype(BF), onehot_ref[...])
        return carry

    lax.fori_loop(0, elements // TILE, tile_step, 0)

    def by_component(first, width):
        rows = []
        for comp in range(3):
            rows.append(jnp.concatenate(
                [acc_ref[block * 24 + comp * 8:block * 24 + comp * 8 + 8, first:first + width]
                 for block in range(blocks)], 0))
        return jnp.concatenate(rows, 1)

    for chunk in range(nodes // 128):
        low = by_component(chunk * 128, 128).astype(BF)
        back = rows_dot(low, sort).astype(BF)
        pieces_ref[2 * chunk] = back[:, :192]
        pieces_ref[2 * chunk + 1] = back[:, 192:]
    rows = []
    for comp in range(3):
        rows.append(jnp.concatenate(
            [acc_ref[block * 24 + comp * 8:block * 24 + comp * 8 + 8, nodes:all_nodes] for block in range(blocks)], 0))
    total = jnp.zeros((samples, shared), F32)
    for comp in range(3):
        place = jnp.where(iota((sep_nodes, shared), 1) == 3 * iota((sep_nodes, shared), 0) + comp, 1.0, 0.0).astype(BF)
        high = rows[comp].astype(BF)
        rest = (rows[comp] - high.astype(F32)).astype(BF)
        total = total + plain_dot(high, place) + plain_dot(rest, place)
    sep_ref[...] = total


def assemble(shared, modulus, connectivity, table, kron, pieces):
    samples, width = shared.shape
    nodes = table.shape[1]
    all_nodes = nodes + width // 3
    whole = pl.BlockSpec(memory_space=pltpu.VMEM)
    far = pl.BlockSpec(memory_space=pl.ANY)
    return pl.pallas_call(
        element_kernel,
        in_specs=[whole, far, far, whole, whole],
        out_shape=(
            jax.ShapeDtypeStruct((pieces, samples, 3 * nodes // pieces), BF),
            jax.ShapeDtypeStruct((samples, width), F32),
        ),
        scratch_shapes=[
            pltpu.VMEM(modulus.shape, F32),
            pltpu.VMEM(connectivity.shape, jnp.int32),
            pltpu.VMEM((3 * samples, nodes + 128), BF),
            pltpu.VMEM((all_nodes, 8 * TILE), BF),
            pltpu.VMEM((3 * samples, 8 * TILE), F32),
            pltpu.VMEM((3 * samples, 8 * TILE), F32),
            pltpu.VMEM((3 * samples, all_nodes), F32),
            pltpu.SemaphoreType.DMA,
            pltpu.SemaphoreType.DMA,
        ],
        compiler_params=pltpu.CompilerParams(vmem_limit_bytes=48 << 20),
        name="elements",
    )(shared, modulus, connectivity, table, kron)


def near_kernel(terms_ref, band_hbm, q_ref, part_ref, band_ref, last_ref, band_sem, last_sem):
    split = last_ref.shape[1]
    begin = band_hbm.shape[1] - split
    band_copy = fetch(band_hbm.at[:, :band_ref.shape[1]], band_ref, band_sem)
    last_copy = fetch(band_hbm.at[:, begin:], last_ref, last_sem)
    near, samples, width = terms_ref.shape
    half = near * width // 4
    terms = terms_ref[...].astype(F32)
    q1 = jnp.concatenate([terms[2 * k] + terms[2 * k + 1] for k in range(near // 2)], 1)
    q_ref[0] = q1
    low = q1.astype(BF)
    band_copy.wait()
    q2 = -jnp.concatenate(
        [plain_dot(low[:, :half], band_ref[:half, :half]), plain_dot(low[:, half:], band_ref[half:2 * half, :half])], 1)
    q_ref[1] = q2
    q3 = -plain_dot(q2.astype(BF), band_ref[:, half:3 * half])
    q_ref[2] = q3
    last_copy.wait()
    offset = 3 * half - begin
    part_ref[...] = (-plain_dot(q3.astype(BF), last_ref[:, offset:offset + 4 * half])).astype(BF)


def near_levels(terms, bands):
    near, samples, width = terms.shape
    columns = near * width // 2
    lead = -(-(3 * columns // 2) // 128) * 128
    tail = bands.shape[1] - 3 * columns // 2 // 128 * 128
    return pl.pallas_call(
        near_kernel,
        in_specs=[pl.BlockSpec(memory_space=pltpu.VMEM), pl.BlockSpec(memory_space=pl.ANY)],
        scratch_shapes=[
            pltpu.VMEM((columns, lead), BF),
            pltpu.VMEM((columns, tail), BF),
            pltpu.SemaphoreType.DMA,
            pltpu.SemaphoreType.DMA,
        ],
        out_shape=(
            jax.ShapeDtypeStruct((3, samples, columns), F32),
            jax.ShapeDtypeStruct((samples, 2 * columns), BF),
        ),
        compiler_params=pltpu.CompilerParams(vmem_limit_bytes=16 << 20),
        name="near_levels",
    )(terms, bands)


def far_kernel(front5_ref, z4_ref, z_ref, ring_hbm, band_ref, x4_ref, x_ref, ring_ref, upper_sem, lower_sem):
    half = band_ref.shape[0] // 2
    middle = ring_ref.shape[0] // 2
    upper = fetch(ring_hbm.at[:middle], ring_ref.at[:middle], upper_sem)
    lower = fetch(ring_hbm.at[middle:], ring_ref.at[middle:], lower_sem)
    upper.wait()
    first = rows_dot(front5_ref[...], ring_ref[:middle])
    lower.wait()
    x4 = z4_ref[...].astype(F32) - jnp.concatenate([first, rows_dot(front5_ref[...], ring_ref[middle:])], 1)
    x4_ref[...] = x4
    x3 = z_ref[2].astype(F32) - rows_dot(x4.astype(BF), band_ref[:, 3 * half:7 * half])
    x_ref[2] = x3
    x2 = z_ref[1].astype(F32) - rows_dot(x3.astype(BF), band_ref[:, half:3 * half])
    x_ref[1] = x2
    low = x2.astype(BF)
    x_ref[0] = z_ref[0].astype(F32) - jnp.concatenate(
        [rows_dot(low[:, :half], band_ref[:half, :half]), rows_dot(low[:, half:], band_ref[half:, :half])], 1)


def far_levels(front5, z4, z_near, ring_band, bands):
    whole = pl.BlockSpec(memory_space=pltpu.VMEM)
    return pl.pallas_call(
        far_kernel,
        in_specs=[whole, whole, whole, pl.BlockSpec(memory_space=pl.ANY), whole],
        scratch_shapes=[
            pltpu.VMEM(ring_band.shape, BF),
            pltpu.SemaphoreType.DMA,
            pltpu.SemaphoreType.DMA,
        ],
        out_shape=(
            jax.ShapeDtypeStruct(z4.shape, F32),
            jax.ShapeDtypeStruct(z_near.shape, F32),
        ),
        compiler_params=pltpu.CompilerParams(vmem_limit_bytes=24 << 20),
        name="far_levels",
    )(front5, z4, z_near, ring_band, bands)


def exchange(value, axis, groups=None):
    return lax.all_to_all(value, axis, 0, 0, axis_index_groups=groups, tiled=True)


def group_lists(leaves, height):
    size = 1 << height
    return [[base + i for i in range(size)] for base in range(0, leaves, size)]


def body(
    interior_disp,
    separator_disp,
    modulus,
    connectivity,
    stiffness,
    load,
    leaf_pivot_inv,
    leaf_coupling,
    pivot_inv,
    coupling,
):
    leaves = lax.axis_size("leaf")
    fronts = lax.axis_size("front")
    levels = leaves.bit_length() - 1
    leaf_index = lax.axis_index("leaf")
    samples, inner_size = interior_disp.shape
    rows = separator_disp.shape[1]
    own_samples = samples // fronts
    pairs = [(source, source ^ 1) for source in range(leaves)]
    partner = lax.ppermute(separator_disp, "leaf", pairs)
    upper_leaf = leaf_index % 2 == 1
    shared = jnp.where(
        upper_leaf,
        jnp.concatenate([partner, separator_disp], 1),
        jnp.concatenate([separator_disp, partner], 1),
    )
    near = 8
    near_cols = -(-rows * (2**5 - 4) // 128) * 128
    near_groups = [[base + i for i in range(near)] for base in range(0, leaves, near)]
    ring_groups = group_lists(leaves, 4)
    spot = leaf_index % near
    near_bands = lax.all_gather(coupling[:, :near_cols], "leaf", axis_index_groups=near_groups)

    def own_coupling(height):
        start = rows * (2**height - 4)
        return coupling[:, start:start + (rows << height)]

    def own_pivot(height):
        start = rows * (2**height - 2)
        return pivot_inv[:, start:start + (rows << height)]

    def joined(stack):
        return jnp.transpose(stack, (1, 0, 2)).reshape(own_samples, -1)

    def split(flat):
        return jnp.transpose(flat.reshape(own_samples, -1, rows), (1, 0, 2))

    def collect(low, height):
        sent = jnp.broadcast_to(low[None], (1 << height,) + low.shape)
        return exchange(sent, "leaf", group_lists(leaves, height))

    table, kron = prepare(interior_disp, stiffness)
    pieces, sep_terms = assemble(shared, modulus, connectivity, table, kron, fronts)
    received = exchange(pieces, "front")
    own_residual = load - jnp.sum(received.astype(F32), 0)
    own_low = own_residual.astype(BF)
    terms = -sep_terms - plain_dot(own_low, leaf_coupling)
    high = lax.reduce_precision(terms, 8, 7)
    both = jnp.concatenate([high, terms - high], 1).astype(BF).reshape(fronts, own_samples, 4 * rows)
    packed = jnp.concatenate([jnp.broadcast_to(own_low[None], (fronts,) + own_low.shape), both], 1)
    everyone = exchange(packed, "front")
    halves = jnp.sum(everyone[:, samples:].astype(F32), 0)
    term = halves[:, :2 * rows] + halves[:, 2 * rows:]
    low_residual = jnp.transpose(everyone[:, :samples], (1, 0, 2)).reshape(samples, inner_size)
    pivoted = own_residual + rows_dot(low_residual, leaf_pivot_inv)

    near_terms = exchange(jnp.broadcast_to(term.astype(BF)[None], (near,) + term.shape), "leaf", near_groups)
    bands = near_bands.reshape(near * rows, near_cols)
    near_q, part4 = near_levels(near_terms, bands)
    start5 = rows * (2**5 - 4)
    ring_band = lax.all_gather(
        lax.optimization_barrier((coupling, part4))[0][:, start5:2 * start5 + 4 * rows], "leaf",
        axis_index_groups=ring_groups,
    ).reshape(16 * rows, 32 * rows)
    q1, q2, q3 = near_q[0], near_q[1], near_q[2]
    low1, low2, low3 = q1.astype(BF), q2.astype(BF), q3.astype(BF)
    ring = 16
    across = []
    for source in range(leaves):
        place = source % ring
        other = place + (12 if place < 4 else -12 if place >= 12 else 4 if place < 8 else -4)
        across.append((source, source - place + other))
    q4 = part4.astype(F32) + lax.ppermute(part4, "leaf", across).astype(F32)
    low4 = q4.astype(BF)

    def piece(flat, index):
        return lax.dynamic_slice_in_dim(flat, index * rows, rows, 1)

    z_own = []
    for height, (value, low) in enumerate(((q1, low1), (q2, low2), (q3, low3)), 1):
        size = 1 << height
        front = lax.dynamic_slice_in_dim(low, spot // size * (size * rows), size * rows, 1)
        z_own.append(piece(value, spot) + rows_dot(front, own_pivot(height)))
    ring_spot = leaf_index % ring
    z4 = piece(q4, ring_spot) + rows_dot(low4, own_pivot(4))
    part5 = -plain_dot(piece(low4, ring_spot), own_coupling(5))
    q5 = jnp.sum(exchange(split(part5.astype(BF)), "leaf", group_lists(leaves, 5)).astype(F32), 0)
    low5 = q5.astype(BF)
    part6 = -plain_dot(low5, own_coupling(6))
    sent = jnp.concatenate(
        [split(part6.astype(BF)), jnp.broadcast_to(low5[None], (leaves,) + low5.shape)], 2)
    back = exchange(sent, "leaf")
    q6 = jnp.sum(back[:, :, :rows].astype(F32), 0)
    full5 = joined(lax.dynamic_slice_in_dim(back, leaf_index // 32 * 32, 32, 0)[:, :, rows:])
    z5 = q5 + rows_dot(full5, own_pivot(5))
    x6 = q6 + rows_dot(joined(collect(q6.astype(BF), 6)), own_pivot(6))
    x5 = z5 - rows_dot(joined(collect(x6.astype(BF), 6)), own_coupling(6))
    packed5 = jnp.concatenate([x5, z4] + z_own, 1).astype(BF)
    packed5, ring_band = lax.optimization_barrier((packed5, ring_band))
    last = collect(packed5, 5)
    same_ring = lax.dynamic_slice_in_dim(last, leaf_index % 32 // 16 * 16, 16, 0)
    nearby = lax.dynamic_slice_in_dim(last, leaf_index % 32 // near * near, near, 0)
    z_near = jnp.transpose(
        nearby[:, :, 2 * rows:].reshape(near, own_samples, 3, rows), (2, 1, 0, 3)
    ).reshape(3, own_samples, near * rows)
    x4_full, x_near = far_levels(
        joined(last[:, :, :rows]), joined(same_ring[:, :, rows:2 * rows]), z_near, ring_band, bands)
    x4 = piece(x4_full, ring_spot)
    x1, x2, x3 = x_near[0], x_near[1], x_near[2]
    corrections = [piece(x1, spot), piece(x2, spot), piece(x3, spot), x4, x5, x6]
    front_low = lax.dynamic_slice_in_dim(x1.astype(BF), spot // 2 * (2 * rows), 2 * rows, 1)
    all_samples = exchange(jnp.broadcast_to(front_low[None], (fronts,) + front_low.shape), "front")
    leaf_correction = pivoted - rows_dot(all_samples.reshape(samples, 2 * rows), leaf_coupling)
    return (leaf_correction, jnp.concatenate(corrections, 1))


def solution(mesh):
    in_specs = (
        P(None, "leaf"),
        P(None, "leaf"),
        P(None, ("leaf", "front")),
        P(None, ("leaf", "front")),
        P(),
        P(None, ("leaf", "front")),
        P(("leaf", "front"), None),
        P(("leaf", "front"), None),
        P("leaf", None),
        P("leaf", None),
    )
    out_specs = (P(None, ("leaf", "front")), P("front", "leaf"))
    return jax.shard_map(body, mesh=mesh, in_specs=in_specs, out_specs=out_specs, check_vma=False)
```

```python
import jax
import jax.numpy as jnp
from jax import lax
from jax.experimental import pallas as pl
from jax.experimental.pallas import tpu as pltpu
from jax.sharding import PartitionSpec as P

BF = jnp.bfloat16
F32 = jnp.float32
ROW_CONTRACT = (((1,), (1,)), ((), ()))
TILE = 1024
ZIGZAG = (0, 2, 4, 6, 7, 5, 3, 1)


def rows_dot(left, right):
    return lax.dot_general(left, right, ROW_CONTRACT, preferred_element_type=F32)


def plain_dot(left, right):
    return jnp.dot(left, right, preferred_element_type=F32)


def iota(shape, dim):
    return lax.broadcasted_iota(jnp.int32, shape, dim)


def spread(components, nodes):
    size = components * nodes
    column = iota((size, size), 1)
    comp = sum((column >= nodes * k).astype(jnp.int32) for k in range(1, components))
    return jnp.where(iota((size, size), 0) == components * (column - comp * nodes) + comp, 1.0, 0.0).astype(BF)


def fetch(source, target, semaphore):
    copy = pltpu.make_async_copy(source, target, semaphore)
    copy.start()
    return copy


def prepare_kernel(disp_hbm, stiff_hbm, table_ref, kron_ref, disp_ref, stiff_ref, disp_sem, stiff_sem):
    disp_copy = fetch(disp_hbm, disp_ref, disp_sem)
    stiff_copy = fetch(stiff_hbm, stiff_ref, stiff_sem)
    samples, inner = disp_ref.shape
    blocks = samples // 8
    sort = spread(3, 128)
    up = jnp.where((iota((192, 24), 0) >> 3) == iota((192, 24), 1), 1.0, 0.0).astype(BF)
    same = (iota((192, 192), 0) & 7) == (iota((192, 192), 1) & 7)
    stiff_copy.wait()
    wide = rows_dot(plain_dot(up, stiff_ref[...].astype(BF)).astype(BF), up)
    kron_ref[...] = jnp.where(same, wide, 0.0).astype(BF)
    disp_copy.wait()
    for chunk in range(inner // 384):
        part = plain_dot(disp_ref[:, chunk * 384:(chunk + 1) * 384].astype(BF), sort)
        rows = [
            part[block * 8:block * 8 + 8, comp * 128:(comp + 1) * 128]
            for block in range(blocks) for comp in range(3)
        ]
        table_ref[:, chunk * 128:(chunk + 1) * 128] = jnp.concatenate(rows, 0).astype(BF)


def prepare(disp, stiffness):
    samples, inner = disp.shape
    return pl.pallas_call(
        prepare_kernel,
        in_specs=[pl.BlockSpec(memory_space=pltpu.HBM), pl.BlockSpec(memory_space=pltpu.HBM)],
        out_shape=(
            jax.ShapeDtypeStruct((3 * samples, inner // 3), BF),
            jax.ShapeDtypeStruct((192, 192), BF),
        ),
        scratch_shapes=[
            pltpu.VMEM(disp.shape, F32),
            pltpu.VMEM(stiffness.shape, F32),
            pltpu.SemaphoreType.DMA,
            pltpu.SemaphoreType.DMA,
        ],
        compiler_params=pltpu.CompilerParams(vmem_limit_bytes=16 << 20),
        name="prepare",
    )(disp, stiffness)


def element_kernel(shared_ref, modulus_hbm, conn_hbm, inner_table_ref, kron_ref, pieces_ref, sep_ref,
                   modulus_ref, conn_ref, table_ref, onehot_ref, gather_ref, force_ref, acc_ref,
                   modulus_sem, conn_sem):
    conn_copy = fetch(conn_hbm, conn_ref, conn_sem)
    modulus_copy = fetch(modulus_hbm, modulus_ref, modulus_sem)
    samples, shared = shared_ref.shape
    elements = conn_ref.shape[1]
    nodes = inner_table_ref.shape[1]
    sep_nodes = shared // 3
    all_nodes = nodes + sep_nodes
    blocks = samples // 8
    sort = spread(3, 128)
    table_ref[:, :nodes] = inner_table_ref[...]
    column = iota((shared, 384), 1)
    comp_of = (column >= 128).astype(jnp.int32) + (column >= 256).astype(jnp.int32)
    local = column - 128 * comp_of
    sep_sort = jnp.where((iota((shared, 384), 0) == 3 * local + comp_of) & (local < sep_nodes), 1.0, 0.0).astype(BF)
    part = plain_dot(shared_ref[...].astype(BF), sep_sort)
    rows = [
        part[block * 8:block * 8 + 8, comp * 128:(comp + 1) * 128] for block in range(blocks) for comp in range(3)
    ]
    table_ref[:, nodes:] = jnp.concatenate(rows, 0).astype(BF)
    table = table_ref[:, :all_nodes]
    conn_copy.wait()
    modulus_copy.wait()
    acc_ref[...] = jnp.zeros_like(acc_ref)

    def tile_step(tile, carry):
        start = pl.multiple_of(tile * TILE, TILE)
        node_row = iota((all_nodes, TILE), 0)
        for corner in range(8):
            which = conn_ref[corner:corner + 1, pl.ds(start, TILE)]
            onehot_ref[:, corner * TILE:(corner + 1) * TILE] = jnp.where(
                node_row == which, 1.0, 0.0).astype(BF)
        for corner in range(8):
            gather_ref[:, corner * TILE:(corner + 1) * TILE] = plain_dot(
                table, onehot_ref[:, corner * TILE:(corner + 1) * TILE])
        for block in range(blocks):
            corners = jnp.concatenate(
                [gather_ref[block * 24:block * 24 + 24, corner * TILE:(corner + 1) * TILE] for corner in range(8)],
                0).astype(BF)
            forces = plain_dot(kron_ref[...], corners)
            scale = modulus_ref[block * 8:block * 8 + 8, pl.ds(start, TILE)]
            forces = forces.reshape(24, 8, TILE) * scale[None]
            forces = forces.reshape(192, TILE)
            for corner in range(8):
                force_ref[block * 24:block * 24 + 24, corner * TILE:(corner + 1) * TILE] = forces[
                    corner * 24:corner * 24 + 24]
        acc_ref[...] += rows_dot(force_ref[...].astype(BF), onehot_ref[...])
        return carry

    lax.fori_loop(0, elements // TILE, tile_step, 0)

    def by_component(first, width):
        rows = []
        for comp in range(3):
            rows.append(jnp.concatenate(
                [acc_ref[block * 24 + comp * 8:block * 24 + comp * 8 + 8, first:first + width]
                 for block in range(blocks)], 0))
        return jnp.concatenate(rows, 1)

    for chunk in range(nodes // 128):
        low = by_component(chunk * 128, 128).astype(BF)
        back = rows_dot(low, sort).astype(BF)
        pieces_ref[2 * chunk] = back[:, :192]
        pieces_ref[2 * chunk + 1] = back[:, 192:]
    rows = []
    for comp in range(3):
        rows.append(jnp.concatenate(
            [acc_ref[block * 24 + comp * 8:block * 24 + comp * 8 + 8, nodes:all_nodes] for block in range(blocks)], 0))
    total = jnp.zeros((samples, shared), F32)
    for comp in range(3):
        place = jnp.where(iota((sep_nodes, shared), 1) == 3 * iota((sep_nodes, shared), 0) + comp, 1.0, 0.0).astype(BF)
        high = rows[comp].astype(BF)
        rest = (rows[comp] - high.astype(F32)).astype(BF)
        total = total + plain_dot(high, place) + plain_dot(rest, place)
    sep_ref[...] = total


def assemble(shared, modulus, connectivity, table, kron, pieces):
    samples, width = shared.shape
    nodes = table.shape[1]
    all_nodes = nodes + width // 3
    whole = pl.BlockSpec(memory_space=pltpu.VMEM)
    far = pl.BlockSpec(memory_space=pltpu.HBM)
    return pl.pallas_call(
        element_kernel,
        in_specs=[whole, far, far, whole, whole],
        out_shape=(
            jax.ShapeDtypeStruct((pieces, samples, 3 * nodes // pieces), BF),
            jax.ShapeDtypeStruct((samples, width), F32),
        ),
        scratch_shapes=[
            pltpu.VMEM(modulus.shape, F32),
            pltpu.VMEM(connectivity.shape, jnp.int32),
            pltpu.VMEM((3 * samples, nodes + 128), BF),
            pltpu.VMEM((all_nodes, 8 * TILE), BF),
            pltpu.VMEM((3 * samples, 8 * TILE), F32),
            pltpu.VMEM((3 * samples, 8 * TILE), F32),
            pltpu.VMEM((3 * samples, all_nodes), F32),
            pltpu.SemaphoreType.DMA,
            pltpu.SemaphoreType.DMA,
        ],
        compiler_params=pltpu.CompilerParams(vmem_limit_bytes=48 << 20),
        name="elements",
    )(shared, modulus, connectivity, table, kron)


def fetch_leaves(source, begin, target, semaphores):
    height = target.shape[0] // len(ZIGZAG)
    width = target.shape[1]
    return [
        fetch(source.at[at * height:(at + 1) * height, begin:begin + width],
              target.at[leaf * height:(leaf + 1) * height], semaphores.at[at])
        for at, leaf in enumerate(ZIGZAG)
    ]


def crop_kernel(source, target, semaphore):
    fetch(source.at[:, :target.shape[1]], target, semaphore).wait()


def crop(array, columns):
    return pl.pallas_call(
        crop_kernel,
        in_specs=[pl.BlockSpec(memory_space=pltpu.HBM)],
        out_specs=pl.BlockSpec(memory_space=pltpu.HBM),
        out_shape=jax.ShapeDtypeStruct((array.shape[0], columns), array.dtype),
        scratch_shapes=[pltpu.SemaphoreType.DMA],
        name="crop",
    )(array)


def near_kernel(terms_ref, band_hbm, q_ref, part_ref, band_ref, last_ref, band_sem, last_sem):
    split = last_ref.shape[1]
    begin = band_hbm.shape[1] - split
    near, samples, width = terms_ref.shape
    band_copies = fetch_leaves(band_hbm, 0, band_ref, band_sem)
    last_copies = fetch_leaves(band_hbm, begin, last_ref, last_sem)
    half = near * width // 4
    terms = terms_ref[...].astype(F32)
    q1 = jnp.concatenate([terms[2 * k] + terms[2 * k + 1] for k in range(near // 2)], 1)
    q_ref[0] = q1
    low = q1.astype(BF)
    for copy in band_copies:
        copy.wait()
    q2 = -jnp.concatenate(
        [plain_dot(low[:, :half], band_ref[:half, :half]), plain_dot(low[:, half:], band_ref[half:2 * half, :half])], 1)
    q_ref[1] = q2
    q3 = -plain_dot(q2.astype(BF), band_ref[:, half:3 * half])
    q_ref[2] = q3
    for copy in last_copies:
        copy.wait()
    offset = 3 * half - begin
    part_ref[...] = (-plain_dot(q3.astype(BF), last_ref[:, offset:offset + 4 * half])).astype(BF)


def near_levels(terms, bands):
    near, samples, width = terms.shape
    columns = near * width // 2
    lead = -(-(3 * columns // 2) // 128) * 128
    tail = bands.shape[1] - 3 * columns // 2 // 128 * 128
    return pl.pallas_call(
        near_kernel,
        in_specs=[pl.BlockSpec(memory_space=pltpu.VMEM), pl.BlockSpec(memory_space=pltpu.HBM)],
        scratch_shapes=[
            pltpu.VMEM((columns, lead), BF),
            pltpu.VMEM((columns, tail), BF),
            pltpu.SemaphoreType.DMA((near,)),
            pltpu.SemaphoreType.DMA((near,)),
        ],
        out_shape=(
            jax.ShapeDtypeStruct((3, samples, columns), F32),
            jax.ShapeDtypeStruct((samples, 2 * columns), BF),
        ),
        compiler_params=pltpu.CompilerParams(vmem_limit_bytes=16 << 20),
        name="near_levels",
    )(terms, bands)


def far_kernel(front5_ref, z4_ref, z_ref, ring_hbm, band_hbm, x4_ref, x_ref, ring_ref, band_ref,
               upper_sem, lower_sem, band_sem):
    half = band_ref.shape[0] // 2
    middle = ring_ref.shape[0] // 2
    upper = fetch(ring_hbm.at[:middle], ring_ref.at[:middle], upper_sem)
    lower = fetch(ring_hbm.at[middle:], ring_ref.at[middle:], lower_sem)
    band_copies = fetch_leaves(band_hbm, 0, band_ref, band_sem)
    upper.wait()
    first = rows_dot(front5_ref[...], ring_ref[:middle])
    lower.wait()
    x4 = z4_ref[...].astype(F32) - jnp.concatenate([first, rows_dot(front5_ref[...], ring_ref[middle:])], 1)
    x4_ref[...] = x4
    for copy in band_copies:
        copy.wait()
    x3 = z_ref[2].astype(F32) - rows_dot(x4.astype(BF), band_ref[:, 3 * half:7 * half])
    x_ref[2] = x3
    x2 = z_ref[1].astype(F32) - rows_dot(x3.astype(BF), band_ref[:, half:3 * half])
    x_ref[1] = x2
    low = x2.astype(BF)
    x_ref[0] = z_ref[0].astype(F32) - jnp.concatenate(
        [rows_dot(low[:, :half], band_ref[:half, :half]), rows_dot(low[:, half:], band_ref[half:, :half])], 1)


def far_levels(front5, z4, z_near, ring_band, bands):
    whole = pl.BlockSpec(memory_space=pltpu.VMEM)
    return pl.pallas_call(
        far_kernel,
        in_specs=[whole, whole, whole] + [pl.BlockSpec(memory_space=pltpu.HBM)] * 2,
        scratch_shapes=[
            pltpu.VMEM(ring_band.shape, BF),
            pltpu.VMEM(bands.shape, BF),
            pltpu.SemaphoreType.DMA,
            pltpu.SemaphoreType.DMA,
            pltpu.SemaphoreType.DMA((len(ZIGZAG),)),
        ],
        out_shape=(
            jax.ShapeDtypeStruct(z4.shape, F32),
            jax.ShapeDtypeStruct(z_near.shape, F32),
        ),
        compiler_params=pltpu.CompilerParams(vmem_limit_bytes=24 << 20),
        name="far_levels",
    )(front5, z4, z_near, ring_band, bands)


def exchange(value, axis, groups=None):
    return lax.all_to_all(value, axis, 0, 0, axis_index_groups=groups, tiled=True)


def group_lists(leaves, height):
    size = 1 << height
    return [[base + i for i in range(size)] for base in range(0, leaves, size)]


def body(
    interior_disp,
    separator_disp,
    modulus,
    connectivity,
    stiffness,
    load,
    leaf_pivot_inv,
    leaf_coupling,
    pivot_inv,
    coupling,
):
    leaves = lax.axis_size("leaf")
    fronts = lax.axis_size("front")
    levels = leaves.bit_length() - 1
    leaf_index = lax.axis_index("leaf")
    samples, inner_size = interior_disp.shape
    rows = separator_disp.shape[1]
    own_samples = samples // fronts
    pairs = [(source, source ^ 1) for source in range(leaves)]
    partner = lax.ppermute(separator_disp, "leaf", pairs)
    upper_leaf = leaf_index % 2 == 1
    shared = jnp.where(
        upper_leaf,
        jnp.concatenate([partner, separator_disp], 1),
        jnp.concatenate([separator_disp, partner], 1),
    )
    near = 8
    near_cols = -(-rows * (2**5 - 4) // 128) * 128
    near_groups = [[base + i for i in range(near)] for base in range(0, leaves, near)]
    ring_groups = group_lists(leaves, 4)
    spot = leaf_index % near
    zigzag_groups = [[base + at for at in ZIGZAG] for base in range(0, leaves, near)]
    near_bands = lax.all_gather(crop(coupling, near_cols), "leaf", axis_index_groups=zigzag_groups)

    def own_coupling(height):
        start = rows * (2**height - 4)
        return coupling[:, start:start + (rows << height)]

    def own_pivot(height):
        start = rows * (2**height - 2)
        return pivot_inv[:, start:start + (rows << height)]

    def joined(stack):
        return jnp.transpose(stack, (1, 0, 2)).reshape(own_samples, -1)

    def split(flat):
        return jnp.transpose(flat.reshape(own_samples, -1, rows), (1, 0, 2))

    def collect(low, height):
        sent = jnp.broadcast_to(low[None], (1 << height,) + low.shape)
        return exchange(sent, "leaf", group_lists(leaves, height))

    table, kron = prepare(interior_disp, stiffness)
    pieces, sep_terms = assemble(shared, modulus, connectivity, table, kron, fronts)
    received = exchange(pieces, "front")
    own_residual = load - jnp.sum(received.astype(F32), 0)
    own_low = own_residual.astype(BF)
    terms = -sep_terms - plain_dot(own_low, leaf_coupling)
    high = lax.reduce_precision(terms, 8, 7)
    both = jnp.concatenate([high, terms - high], 1).astype(BF).reshape(fronts, own_samples, 4 * rows)
    packed = jnp.concatenate([jnp.broadcast_to(own_low[None], (fronts,) + own_low.shape), both], 1)
    everyone = exchange(packed, "front")
    halves = jnp.sum(everyone[:, samples:].astype(F32), 0)
    term = halves[:, :2 * rows] + halves[:, 2 * rows:]
    low_residual = jnp.transpose(everyone[:, :samples], (1, 0, 2)).reshape(samples, inner_size)
    pivoted = own_residual + rows_dot(low_residual, leaf_pivot_inv)

    near_terms = exchange(jnp.broadcast_to(term.astype(BF)[None], (near,) + term.shape), "leaf", near_groups)
    bands = near_bands.reshape(near * rows, near_cols)
    near_q, part4 = near_levels(near_terms, bands)
    start5 = rows * (2**5 - 4)
    ring_band = lax.all_gather(
        lax.optimization_barrier((coupling, part4))[0][:, start5:2 * start5 + 4 * rows], "leaf",
        axis_index_groups=ring_groups,
    ).reshape(16 * rows, 32 * rows)
    q1, q2, q3 = near_q[0], near_q[1], near_q[2]
    low1, low2, low3 = q1.astype(BF), q2.astype(BF), q3.astype(BF)
    ring = 16
    across = []
    for source in range(leaves):
        place = source % ring
        other = place + (12 if place < 4 else -12 if place >= 12 else 4 if place < 8 else -4)
        across.append((source, source - place + other))
    q4 = part4.astype(F32) + lax.ppermute(part4, "leaf", across).astype(F32)
    low4 = q4.astype(BF)

    def piece(flat, index):
        return lax.dynamic_slice_in_dim(flat, index * rows, rows, 1)

    z_own = []
    for height, (value, low) in enumerate(((q1, low1), (q2, low2), (q3, low3)), 1):
        size = 1 << height
        front = lax.dynamic_slice_in_dim(low, spot // size * (size * rows), size * rows, 1)
        z_own.append(piece(value, spot) + rows_dot(front, own_pivot(height)))
    ring_spot = leaf_index % ring
    z4 = piece(q4, ring_spot) + rows_dot(low4, own_pivot(4))
    part5 = -plain_dot(piece(low4, ring_spot), own_coupling(5))
    q5 = jnp.sum(exchange(split(part5.astype(BF)), "leaf", group_lists(leaves, 5)).astype(F32), 0)
    low5 = q5.astype(BF)
    part6 = -plain_dot(low5, own_coupling(6))
    sent = jnp.concatenate(
        [split(part6.astype(BF)), jnp.broadcast_to(low5[None], (leaves,) + low5.shape)], 2)
    back = exchange(sent, "leaf")
    q6 = jnp.sum(back[:, :, :rows].astype(F32), 0)
    full5 = joined(lax.dynamic_slice_in_dim(back, leaf_index // 32 * 32, 32, 0)[:, :, rows:])
    z5 = q5 + rows_dot(full5, own_pivot(5))
    x6 = q6 + rows_dot(joined(collect(q6.astype(BF), 6)), own_pivot(6))
    x5 = z5 - rows_dot(joined(collect(x6.astype(BF), 6)), own_coupling(6))
    packed5 = jnp.concatenate([x5, z4] + z_own, 1).astype(BF)
    packed5, ring_band = lax.optimization_barrier((packed5, ring_band))
    last = collect(packed5, 5)
    same_ring = lax.dynamic_slice_in_dim(last, leaf_index % 32 // 16 * 16, 16, 0)
    nearby = lax.dynamic_slice_in_dim(last, leaf_index % 32 // near * near, near, 0)
    z_near = jnp.transpose(
        nearby[:, :, 2 * rows:].reshape(near, own_samples, 3, rows), (2, 1, 0, 3)
    ).reshape(3, own_samples, near * rows)
    x4_full, x_near = far_levels(
        joined(last[:, :, :rows]), joined(same_ring[:, :, rows:2 * rows]), z_near, ring_band, bands)
    x4 = piece(x4_full, ring_spot)
    x1, x2, x3 = x_near[0], x_near[1], x_near[2]
    corrections = [piece(x1, spot), piece(x2, spot), piece(x3, spot), x4, x5, x6]
    front_low = lax.dynamic_slice_in_dim(x1.astype(BF), spot // 2 * (2 * rows), 2 * rows, 1)
    all_samples = exchange(jnp.broadcast_to(front_low[None], (fronts,) + front_low.shape), "front")
    leaf_correction = pivoted - rows_dot(all_samples.reshape(samples, 2 * rows), leaf_coupling)
    return (leaf_correction, jnp.concatenate(corrections, 1))


def solution(mesh):
    in_specs = (
        P(None, "leaf"),
        P(None, "leaf"),
        P(None, ("leaf", "front")),
        P(None, ("leaf", "front")),
        P(),
        P(None, ("leaf", "front")),
        P(("leaf", "front"), None),
        P(("leaf", "front"), None),
        P("leaf", None),
        P("leaf", None),
    )
    out_specs = (P(None, ("leaf", "front")), P("front", "leaf"))
    return jax.shard_map(body, mesh=mesh, in_specs=in_specs, out_specs=out_specs, check_vma=False)
```

```python
import jax
import jax.numpy as jnp
from jax import lax
from jax.experimental import pallas as pl
from jax.experimental.pallas import tpu as pltpu
from jax.sharding import PartitionSpec as P

BF = jnp.bfloat16
F32 = jnp.float32
ROW_CONTRACT = (((1,), (1,)), ((), ()))
TILE = 1024
ZIGZAG = (0, 2, 4, 6, 7, 5, 3, 1)


def rows_dot(left, right):
    return lax.dot_general(left, right, ROW_CONTRACT, preferred_element_type=F32)


def plain_dot(left, right):
    return jnp.dot(left, right, preferred_element_type=F32)


def iota(shape, dim):
    return lax.broadcasted_iota(jnp.int32, shape, dim)


def spread(components, nodes):
    size = components * nodes
    column = iota((size, size), 1)
    comp = sum((column >= nodes * k).astype(jnp.int32) for k in range(1, components))
    return jnp.where(iota((size, size), 0) == components * (column - comp * nodes) + comp, 1.0, 0.0).astype(BF)


def fetch(source, target, semaphore):
    copy = pltpu.make_async_copy(source, target, semaphore)
    copy.start()
    return copy


def prepare_kernel(disp_hbm, stiff_hbm, table_ref, kron_ref, disp_ref, stiff_ref, disp_sem, stiff_sem):
    disp_copy = fetch(disp_hbm, disp_ref, disp_sem)
    stiff_copy = fetch(stiff_hbm, stiff_ref, stiff_sem)
    samples, inner = disp_ref.shape
    blocks = samples // 8
    sort = spread(3, 128)
    up = jnp.where((iota((192, 24), 0) >> 3) == iota((192, 24), 1), 1.0, 0.0).astype(BF)
    same = (iota((192, 192), 0) & 7) == (iota((192, 192), 1) & 7)
    stiff_copy.wait()
    wide = rows_dot(plain_dot(up, stiff_ref[...].astype(BF)).astype(BF), up)
    kron_ref[...] = jnp.where(same, wide, 0.0).astype(BF)
    disp_copy.wait()
    for chunk in range(inner // 384):
        part = plain_dot(disp_ref[:, chunk * 384:(chunk + 1) * 384].astype(BF), sort)
        rows = [
            part[block * 8:block * 8 + 8, comp * 128:(comp + 1) * 128]
            for block in range(blocks) for comp in range(3)
        ]
        table_ref[:, chunk * 128:(chunk + 1) * 128] = jnp.concatenate(rows, 0).astype(BF)


def prepare(disp, stiffness):
    samples, inner = disp.shape
    return pl.pallas_call(
        prepare_kernel,
        in_specs=[pl.BlockSpec(memory_space=pltpu.HBM), pl.BlockSpec(memory_space=pltpu.HBM)],
        out_shape=(
            jax.ShapeDtypeStruct((3 * samples, inner // 3), BF),
            jax.ShapeDtypeStruct((192, 192), BF),
        ),
        scratch_shapes=[
            pltpu.VMEM(disp.shape, F32),
            pltpu.VMEM(stiffness.shape, F32),
            pltpu.SemaphoreType.DMA,
            pltpu.SemaphoreType.DMA,
        ],
        compiler_params=pltpu.CompilerParams(vmem_limit_bytes=16 << 20),
        name="prepare",
    )(resident(disp), resident(stiffness))


def element_kernel(shared_ref, modulus_hbm, conn_hbm, inner_table_ref, kron_ref, pieces_ref, sep_ref,
                   modulus_ref, conn_ref, table_ref, onehot_ref, gather_ref, force_ref, acc_ref,
                   modulus_sem, conn_sem):
    conn_copy = fetch(conn_hbm, conn_ref, conn_sem)
    modulus_copy = fetch(modulus_hbm, modulus_ref, modulus_sem)
    samples, shared = shared_ref.shape
    elements = conn_ref.shape[1]
    nodes = inner_table_ref.shape[1]
    sep_nodes = shared // 3
    all_nodes = nodes + sep_nodes
    blocks = samples // 8
    sort = spread(3, 128)
    table_ref[:, :nodes] = inner_table_ref[...]
    column = iota((shared, 384), 1)
    comp_of = (column >= 128).astype(jnp.int32) + (column >= 256).astype(jnp.int32)
    local = column - 128 * comp_of
    sep_sort = jnp.where((iota((shared, 384), 0) == 3 * local + comp_of) & (local < sep_nodes), 1.0, 0.0).astype(BF)
    part = plain_dot(shared_ref[...].astype(BF), sep_sort)
    rows = [
        part[block * 8:block * 8 + 8, comp * 128:(comp + 1) * 128] for block in range(blocks) for comp in range(3)
    ]
    table_ref[:, nodes:] = jnp.concatenate(rows, 0).astype(BF)
    table = table_ref[:, :all_nodes]
    conn_copy.wait()
    modulus_copy.wait()
    acc_ref[...] = jnp.zeros_like(acc_ref)

    def tile_step(tile, carry):
        start = pl.multiple_of(tile * TILE, TILE)
        node_row = iota((all_nodes, TILE), 0)
        for corner in range(8):
            which = conn_ref[corner:corner + 1, pl.ds(start, TILE)]
            onehot_ref[:, corner * TILE:(corner + 1) * TILE] = jnp.where(
                node_row == which, 1.0, 0.0).astype(BF)
        for corner in range(8):
            gather_ref[:, corner * TILE:(corner + 1) * TILE] = plain_dot(
                table, onehot_ref[:, corner * TILE:(corner + 1) * TILE])
        for block in range(blocks):
            corners = jnp.concatenate(
                [gather_ref[block * 24:block * 24 + 24, corner * TILE:(corner + 1) * TILE] for corner in range(8)],
                0).astype(BF)
            forces = plain_dot(kron_ref[...], corners)
            scale = modulus_ref[block * 8:block * 8 + 8, pl.ds(start, TILE)]
            forces = forces.reshape(24, 8, TILE) * scale[None]
            forces = forces.reshape(192, TILE)
            for corner in range(8):
                force_ref[block * 24:block * 24 + 24, corner * TILE:(corner + 1) * TILE] = forces[
                    corner * 24:corner * 24 + 24]
        acc_ref[...] += rows_dot(force_ref[...].astype(BF), onehot_ref[...])
        return carry

    lax.fori_loop(0, elements // TILE, tile_step, 0)

    def by_component(first, width):
        rows = []
        for comp in range(3):
            rows.append(jnp.concatenate(
                [acc_ref[block * 24 + comp * 8:block * 24 + comp * 8 + 8, first:first + width]
                 for block in range(blocks)], 0))
        return jnp.concatenate(rows, 1)

    for chunk in range(nodes // 128):
        low = by_component(chunk * 128, 128).astype(BF)
        back = rows_dot(low, sort).astype(BF)
        pieces_ref[2 * chunk] = back[:, :192]
        pieces_ref[2 * chunk + 1] = back[:, 192:]
    rows = []
    for comp in range(3):
        rows.append(jnp.concatenate(
            [acc_ref[block * 24 + comp * 8:block * 24 + comp * 8 + 8, nodes:all_nodes] for block in range(blocks)], 0))
    total = jnp.zeros((samples, shared), F32)
    for comp in range(3):
        place = jnp.where(iota((sep_nodes, shared), 1) == 3 * iota((sep_nodes, shared), 0) + comp, 1.0, 0.0).astype(BF)
        high = rows[comp].astype(BF)
        rest = (rows[comp] - high.astype(F32)).astype(BF)
        total = total + plain_dot(high, place) + plain_dot(rest, place)
    sep_ref[...] = total


def assemble(shared, modulus, connectivity, table, kron, pieces):
    samples, width = shared.shape
    nodes = table.shape[1]
    all_nodes = nodes + width // 3
    whole = pl.BlockSpec(memory_space=pltpu.VMEM)
    far = pl.BlockSpec(memory_space=pltpu.HBM)
    return pl.pallas_call(
        element_kernel,
        in_specs=[whole, far, far, whole, whole],
        out_shape=(
            jax.ShapeDtypeStruct((pieces, samples, 3 * nodes // pieces), BF),
            jax.ShapeDtypeStruct((samples, width), F32),
        ),
        scratch_shapes=[
            pltpu.VMEM(modulus.shape, F32),
            pltpu.VMEM(connectivity.shape, jnp.int32),
            pltpu.VMEM((3 * samples, nodes + 128), BF),
            pltpu.VMEM((all_nodes, 8 * TILE), BF),
            pltpu.VMEM((3 * samples, 8 * TILE), F32),
            pltpu.VMEM((3 * samples, 8 * TILE), F32),
            pltpu.VMEM((3 * samples, all_nodes), F32),
            pltpu.SemaphoreType.DMA,
            pltpu.SemaphoreType.DMA,
        ],
        compiler_params=pltpu.CompilerParams(vmem_limit_bytes=48 << 20),
        name="elements",
    )(shared, resident(modulus), resident(connectivity), table, kron)


def fetch_leaves(source, begin, target, semaphores):
    height = target.shape[0] // len(ZIGZAG)
    width = target.shape[1]
    return [
        fetch(source.at[at * height:(at + 1) * height, begin:begin + width],
              target.at[leaf * height:(leaf + 1) * height], semaphores.at[at])
        for at, leaf in enumerate(ZIGZAG)
    ]


def resident(array):
    return pltpu.with_memory_space_constraint(array, pltpu.HBM)


def near_kernel(terms_ref, band_hbm, q_ref, part_ref, band_ref, last_ref, band_sem, last_sem):
    split = last_ref.shape[1]
    begin = band_hbm.shape[1] - split
    near, samples, width = terms_ref.shape
    band_copies = fetch_leaves(band_hbm, 0, band_ref, band_sem)
    last_copies = fetch_leaves(band_hbm, begin, last_ref, last_sem)
    half = near * width // 4
    terms = terms_ref[...].astype(F32)
    q1 = jnp.concatenate([terms[2 * k] + terms[2 * k + 1] for k in range(near // 2)], 1)
    q_ref[0] = q1
    low = q1.astype(BF)
    for copy in band_copies:
        copy.wait()
    q2 = -jnp.concatenate(
        [plain_dot(low[:, :half], band_ref[:half, :half]), plain_dot(low[:, half:], band_ref[half:2 * half, :half])], 1)
    q_ref[1] = q2
    q3 = -plain_dot(q2.astype(BF), band_ref[:, half:3 * half])
    q_ref[2] = q3
    for copy in last_copies:
        copy.wait()
    offset = 3 * half - begin
    part_ref[...] = (-plain_dot(q3.astype(BF), last_ref[:, offset:offset + 4 * half])).astype(BF)


def near_levels(terms, bands):
    near, samples, width = terms.shape
    columns = near * width // 2
    lead = -(-(3 * columns // 2) // 128) * 128
    tail = bands.shape[1] - 3 * columns // 2 // 128 * 128
    return pl.pallas_call(
        near_kernel,
        in_specs=[pl.BlockSpec(memory_space=pltpu.VMEM), pl.BlockSpec(memory_space=pltpu.HBM)],
        scratch_shapes=[
            pltpu.VMEM((columns, lead), BF),
            pltpu.VMEM((columns, tail), BF),
            pltpu.SemaphoreType.DMA((near,)),
            pltpu.SemaphoreType.DMA((near,)),
        ],
        out_shape=(
            jax.ShapeDtypeStruct((3, samples, columns), F32),
            jax.ShapeDtypeStruct((samples, 2 * columns), BF),
        ),
        compiler_params=pltpu.CompilerParams(vmem_limit_bytes=16 << 20),
        name="near_levels",
    )(terms, resident(bands))


def far_kernel(front5_ref, z4_ref, z_ref, ring_hbm, near_ref, x4_ref, x_ref, ring_ref,
               upper_sem, lower_sem):
    half = near_ref.shape[0] // 2
    height = near_ref.shape[0] // len(ZIGZAG)
    middle = ring_ref.shape[0] // 2
    upper = fetch(ring_hbm.at[:middle], ring_ref.at[:middle], upper_sem)
    lower = fetch(ring_hbm.at[middle:], ring_ref.at[middle:], lower_sem)
    upper.wait()
    first = rows_dot(front5_ref[...], ring_ref[:middle])
    lower.wait()
    x4 = z4_ref[...].astype(F32) - jnp.concatenate([first, rows_dot(front5_ref[...], ring_ref[middle:])], 1)
    x4_ref[...] = x4
    places = [ZIGZAG.index(leaf) * height for leaf in range(len(ZIGZAG))]

    def near_rows(first, last, begin, end):
        return jnp.concatenate([near_ref[at:at + height, begin:end] for at in places[first:last]], 0)

    x3 = z_ref[2].astype(F32) - rows_dot(x4.astype(BF), near_rows(0, 8, 3 * half, 7 * half))
    x_ref[2] = x3
    x2 = z_ref[1].astype(F32) - rows_dot(x3.astype(BF), near_rows(0, 8, half, 3 * half))
    x_ref[1] = x2
    low = x2.astype(BF)
    x_ref[0] = z_ref[0].astype(F32) - jnp.concatenate(
        [rows_dot(low[:, :half], near_rows(0, 4, 0, half)), rows_dot(low[:, half:], near_rows(4, 8, 0, half))], 1)


def far_levels(front5, z4, z_near, ring_band, bands):
    whole = pl.BlockSpec(memory_space=pltpu.VMEM)
    return pl.pallas_call(
        far_kernel,
        in_specs=[whole, whole, whole, pl.BlockSpec(memory_space=pltpu.HBM), whole],
        scratch_shapes=[
            pltpu.VMEM(ring_band.shape, BF),
            pltpu.SemaphoreType.DMA,
            pltpu.SemaphoreType.DMA,
        ],
        out_shape=(
            jax.ShapeDtypeStruct(z4.shape, F32),
            jax.ShapeDtypeStruct(z_near.shape, F32),
        ),
        compiler_params=pltpu.CompilerParams(vmem_limit_bytes=24 << 20),
        name="far_levels",
    )(front5, z4, z_near, resident(ring_band), bands)


def exchange(value, axis, groups=None):
    return lax.all_to_all(value, axis, 0, 0, axis_index_groups=groups, tiled=True)


def group_lists(leaves, height):
    size = 1 << height
    return [[base + i for i in range(size)] for base in range(0, leaves, size)]


def body(
    interior_disp,
    separator_disp,
    modulus,
    connectivity,
    stiffness,
    load,
    leaf_pivot_inv,
    leaf_coupling,
    pivot_inv,
    coupling,
):
    leaves = lax.axis_size("leaf")
    fronts = lax.axis_size("front")
    levels = leaves.bit_length() - 1
    leaf_index = lax.axis_index("leaf")
    samples, inner_size = interior_disp.shape
    rows = separator_disp.shape[1]
    own_samples = samples // fronts
    pairs = [(source, source ^ 1) for source in range(leaves)]
    partner = lax.ppermute(separator_disp, "leaf", pairs)
    upper_leaf = leaf_index % 2 == 1
    shared = jnp.where(
        upper_leaf,
        jnp.concatenate([partner, separator_disp], 1),
        jnp.concatenate([separator_disp, partner], 1),
    )
    near = 8
    near_cols = -(-rows * (2**5 - 4) // 128) * 128
    near_groups = [[base + i for i in range(near)] for base in range(0, leaves, near)]
    ring_groups = group_lists(leaves, 4)
    spot = leaf_index % near
    zigzag_groups = [[base + at for at in ZIGZAG] for base in range(0, leaves, near)]
    near_bands = lax.all_gather(coupling[:, :near_cols], "leaf", axis_index_groups=zigzag_groups)

    def own_coupling(height):
        start = rows * (2**height - 4)
        return coupling[:, start:start + (rows << height)]

    def own_pivot(height):
        start = rows * (2**height - 2)
        return pivot_inv[:, start:start + (rows << height)]

    def joined(stack):
        return jnp.transpose(stack, (1, 0, 2)).reshape(own_samples, -1)

    def split(flat):
        return jnp.transpose(flat.reshape(own_samples, -1, rows), (1, 0, 2))

    def collect(low, height):
        sent = jnp.broadcast_to(low[None], (1 << height,) + low.shape)
        return exchange(sent, "leaf", group_lists(leaves, height))

    table, kron = prepare(interior_disp, stiffness)
    pieces, sep_terms = assemble(shared, modulus, connectivity, table, kron, fronts)
    received = exchange(pieces, "front")
    own_residual = load - jnp.sum(received.astype(F32), 0)
    own_low = own_residual.astype(BF)
    terms = -sep_terms - plain_dot(own_low, leaf_coupling)
    high = lax.reduce_precision(terms, 8, 7)
    both = jnp.concatenate([high, terms - high], 1).astype(BF).reshape(fronts, own_samples, 4 * rows)
    packed = jnp.concatenate([jnp.broadcast_to(own_low[None], (fronts,) + own_low.shape), both], 1)
    everyone = exchange(packed, "front")
    halves = jnp.sum(everyone[:, samples:].astype(F32), 0)
    term = halves[:, :2 * rows] + halves[:, 2 * rows:]
    low_residual = jnp.transpose(everyone[:, :samples], (1, 0, 2)).reshape(samples, inner_size)
    pivoted = own_residual + rows_dot(low_residual, leaf_pivot_inv)

    near_terms = exchange(jnp.broadcast_to(term.astype(BF)[None], (near,) + term.shape), "leaf", near_groups)
    bands = near_bands.reshape(near * rows, near_cols)
    near_q, part4 = near_levels(near_terms, bands)
    start5 = rows * (2**5 - 4)
    ring_band = lax.all_gather(
        lax.optimization_barrier((coupling, part4))[0][:, start5:2 * start5 + 4 * rows], "leaf",
        axis_index_groups=ring_groups,
    ).reshape(16 * rows, 32 * rows)
    q1, q2, q3 = near_q[0], near_q[1], near_q[2]
    low1, low2, low3 = q1.astype(BF), q2.astype(BF), q3.astype(BF)
    ring = 16
    across = []
    for source in range(leaves):
        place = source % ring
        other = place + (12 if place < 4 else -12 if place >= 12 else 4 if place < 8 else -4)
        across.append((source, source - place + other))
    q4 = part4.astype(F32) + lax.ppermute(part4, "leaf", across).astype(F32)
    low4 = q4.astype(BF)

    def piece(flat, index):
        return lax.dynamic_slice_in_dim(flat, index * rows, rows, 1)

    z_own = []
    for height, (value, low) in enumerate(((q1, low1), (q2, low2), (q3, low3)), 1):
        size = 1 << height
        front = lax.dynamic_slice_in_dim(low, spot // size * (size * rows), size * rows, 1)
        z_own.append(piece(value, spot) + rows_dot(front, own_pivot(height)))
    ring_spot = leaf_index % ring
    z4 = piece(q4, ring_spot) + rows_dot(low4, own_pivot(4))
    part5 = -plain_dot(piece(low4, ring_spot), own_coupling(5))
    q5 = jnp.sum(exchange(split(part5.astype(BF)), "leaf", group_lists(leaves, 5)).astype(F32), 0)
    low5 = q5.astype(BF)
    part6 = -plain_dot(low5, own_coupling(6))
    sent = jnp.concatenate(
        [split(part6.astype(BF)), jnp.broadcast_to(low5[None], (leaves,) + low5.shape)], 2)
    back = exchange(sent, "leaf")
    q6 = jnp.sum(back[:, :, :rows].astype(F32), 0)
    full5 = joined(lax.dynamic_slice_in_dim(back, leaf_index // 32 * 32, 32, 0)[:, :, rows:])
    z5 = q5 + rows_dot(full5, own_pivot(5))
    x6 = q6 + rows_dot(joined(collect(q6.astype(BF), 6)), own_pivot(6))
    x5 = z5 - rows_dot(joined(collect(x6.astype(BF), 6)), own_coupling(6))
    packed5 = jnp.concatenate([x5, z4] + z_own, 1).astype(BF)
    packed5, ring_band = lax.optimization_barrier((packed5, ring_band))
    last = collect(packed5, 5)
    same_ring = lax.dynamic_slice_in_dim(last, leaf_index % 32 // 16 * 16, 16, 0)
    nearby = lax.dynamic_slice_in_dim(last, leaf_index % 32 // near * near, near, 0)
    z_near = jnp.transpose(
        nearby[:, :, 2 * rows:].reshape(near, own_samples, 3, rows), (2, 1, 0, 3)
    ).reshape(3, own_samples, near * rows)
    x4_full, x_near = far_levels(
        joined(last[:, :, :rows]), joined(same_ring[:, :, rows:2 * rows]), z_near, ring_band, bands)
    x4 = piece(x4_full, ring_spot)
    x1, x2, x3 = x_near[0], x_near[1], x_near[2]
    corrections = [piece(x1, spot), piece(x2, spot), piece(x3, spot), x4, x5, x6]
    front_low = lax.dynamic_slice_in_dim(x1.astype(BF), spot // 2 * (2 * rows), 2 * rows, 1)
    all_samples = exchange(jnp.broadcast_to(front_low[None], (fronts,) + front_low.shape), "front")
    leaf_correction = pivoted - rows_dot(all_samples.reshape(samples, 2 * rows), leaf_coupling)
    return (leaf_correction, jnp.concatenate(corrections, 1))


def solution(mesh):
    in_specs = (
        P(None, "leaf"),
        P(None, "leaf"),
        P(None, ("leaf", "front")),
        P(None, ("leaf", "front")),
        P(),
        P(None, ("leaf", "front")),
        P(("leaf", "front"), None),
        P(("leaf", "front"), None),
        P("leaf", None),
        P("leaf", None),
    )
    out_specs = (P(None, ("leaf", "front")), P("front", "leaf"))
    return jax.shard_map(body, mesh=mesh, in_specs=in_specs, out_specs=out_specs, check_vma=False)
```

```python
import jax
import jax.numpy as jnp
from jax import lax
from jax.experimental import pallas as pl
from jax.experimental.pallas import tpu as pltpu
from jax.sharding import PartitionSpec as P

BF = jnp.bfloat16
F32 = jnp.float32
ROW_CONTRACT = (((1,), (1,)), ((), ()))
TILE = 1024
ZIGZAG = (0, 2, 4, 6, 7, 5, 3, 1)


def rows_dot(left, right):
    return lax.dot_general(left, right, ROW_CONTRACT, preferred_element_type=F32)


def plain_dot(left, right):
    return jnp.dot(left, right, preferred_element_type=F32)


def iota(shape, dim):
    return lax.broadcasted_iota(jnp.int32, shape, dim)


def spread(components, nodes):
    size = components * nodes
    column = iota((size, size), 1)
    comp = sum((column >= nodes * k).astype(jnp.int32) for k in range(1, components))
    return jnp.where(iota((size, size), 0) == components * (column - comp * nodes) + comp, 1.0, 0.0).astype(BF)


def fetch(source, target, semaphore):
    copy = pltpu.make_async_copy(source, target, semaphore)
    copy.start()
    return copy


def prepare_kernel(disp_hbm, stiff_hbm, table_ref, kron_ref, disp_ref, stiff_ref, disp_sem, stiff_sem):
    disp_copy = fetch(disp_hbm, disp_ref, disp_sem)
    stiff_copy = fetch(stiff_hbm, stiff_ref, stiff_sem)
    samples, inner = disp_ref.shape
    blocks = samples // 8
    sort = spread(3, 128)
    up = jnp.where((iota((192, 24), 0) >> 3) == iota((192, 24), 1), 1.0, 0.0).astype(BF)
    same = (iota((192, 192), 0) & 7) == (iota((192, 192), 1) & 7)
    stiff_copy.wait()
    wide = rows_dot(plain_dot(up, stiff_ref[...].astype(BF)).astype(BF), up)
    kron_ref[...] = jnp.where(same, wide, 0.0).astype(BF)
    disp_copy.wait()
    for chunk in range(inner // 384):
        part = plain_dot(disp_ref[:, chunk * 384:(chunk + 1) * 384].astype(BF), sort)
        rows = [
            part[block * 8:block * 8 + 8, comp * 128:(comp + 1) * 128]
            for block in range(blocks) for comp in range(3)
        ]
        table_ref[:, chunk * 128:(chunk + 1) * 128] = jnp.concatenate(rows, 0).astype(BF)


def prepare(disp, stiffness):
    samples, inner = disp.shape
    return pl.pallas_call(
        prepare_kernel,
        in_specs=[pl.BlockSpec(memory_space=pltpu.HBM), pl.BlockSpec(memory_space=pltpu.HBM)],
        out_shape=(
            jax.ShapeDtypeStruct((3 * samples, inner // 3), BF),
            jax.ShapeDtypeStruct((192, 192), BF),
        ),
        scratch_shapes=[
            pltpu.VMEM(disp.shape, F32),
            pltpu.VMEM(stiffness.shape, F32),
            pltpu.SemaphoreType.DMA,
            pltpu.SemaphoreType.DMA,
        ],
        compiler_params=pltpu.CompilerParams(vmem_limit_bytes=16 << 20),
        name="prepare",
    )(resident(disp), resident(stiffness))


def element_kernel(shared_ref, modulus_hbm, conn_hbm, inner_table_ref, kron_ref, pieces_ref, sep_ref,
                   modulus_ref, conn_ref, table_ref, onehot_ref, gather_ref, force_ref, acc_ref,
                   modulus_sem, conn_sem):
    conn_copy = fetch(conn_hbm, conn_ref, conn_sem)
    modulus_copy = fetch(modulus_hbm, modulus_ref, modulus_sem)
    samples, shared = shared_ref.shape
    elements = conn_ref.shape[1]
    nodes = inner_table_ref.shape[1]
    sep_nodes = shared // 3
    all_nodes = nodes + sep_nodes
    blocks = samples // 8
    sort = spread(3, 128)
    table_ref[:, :nodes] = inner_table_ref[...]
    column = iota((shared, 384), 1)
    comp_of = (column >= 128).astype(jnp.int32) + (column >= 256).astype(jnp.int32)
    local = column - 128 * comp_of
    sep_sort = jnp.where((iota((shared, 384), 0) == 3 * local + comp_of) & (local < sep_nodes), 1.0, 0.0).astype(BF)
    part = plain_dot(shared_ref[...].astype(BF), sep_sort)
    rows = [
        part[block * 8:block * 8 + 8, comp * 128:(comp + 1) * 128] for block in range(blocks) for comp in range(3)
    ]
    table_ref[:, nodes:] = jnp.concatenate(rows, 0).astype(BF)
    table = table_ref[:, :all_nodes]
    conn_copy.wait()
    modulus_copy.wait()
    acc_ref[...] = jnp.zeros_like(acc_ref)

    def tile_step(tile, carry):
        start = pl.multiple_of(tile * TILE, TILE)
        node_row = iota((all_nodes, TILE), 0)
        for corner in range(8):
            which = conn_ref[corner:corner + 1, pl.ds(start, TILE)]
            onehot_ref[:, corner * TILE:(corner + 1) * TILE] = jnp.where(
                node_row == which, 1.0, 0.0).astype(BF)
        for corner in range(8):
            gather_ref[:, corner * TILE:(corner + 1) * TILE] = plain_dot(
                table, onehot_ref[:, corner * TILE:(corner + 1) * TILE])
        for block in range(blocks):
            corners = jnp.concatenate(
                [gather_ref[block * 24:block * 24 + 24, corner * TILE:(corner + 1) * TILE] for corner in range(8)],
                0).astype(BF)
            forces = plain_dot(kron_ref[...], corners)
            scale = modulus_ref[block * 8:block * 8 + 8, pl.ds(start, TILE)]
            forces = forces.reshape(24, 8, TILE) * scale[None]
            forces = forces.reshape(192, TILE)
            for corner in range(8):
                force_ref[block * 24:block * 24 + 24, corner * TILE:(corner + 1) * TILE] = forces[
                    corner * 24:corner * 24 + 24]
        acc_ref[...] += rows_dot(force_ref[...].astype(BF), onehot_ref[...])
        return carry

    lax.fori_loop(0, elements // TILE, tile_step, 0)

    def by_component(first, width):
        rows = []
        for comp in range(3):
            rows.append(jnp.concatenate(
                [acc_ref[block * 24 + comp * 8:block * 24 + comp * 8 + 8, first:first + width]
                 for block in range(blocks)], 0))
        return jnp.concatenate(rows, 1)

    for chunk in range(nodes // 128):
        low = by_component(chunk * 128, 128).astype(BF)
        back = rows_dot(low, sort).astype(BF)
        pieces_ref[2 * chunk] = back[:, :192]
        pieces_ref[2 * chunk + 1] = back[:, 192:]
    rows = []
    for comp in range(3):
        rows.append(jnp.concatenate(
            [acc_ref[block * 24 + comp * 8:block * 24 + comp * 8 + 8, nodes:all_nodes] for block in range(blocks)], 0))
    total = jnp.zeros((samples, shared), F32)
    for comp in range(3):
        place = jnp.where(iota((sep_nodes, shared), 1) == 3 * iota((sep_nodes, shared), 0) + comp, 1.0, 0.0).astype(BF)
        high = rows[comp].astype(BF)
        rest = (rows[comp] - high.astype(F32)).astype(BF)
        total = total + plain_dot(high, place) + plain_dot(rest, place)
    sep_ref[...] = total


def assemble(shared, modulus, connectivity, table, kron, pieces):
    samples, width = shared.shape
    nodes = table.shape[1]
    all_nodes = nodes + width // 3
    whole = pl.BlockSpec(memory_space=pltpu.VMEM)
    far = pl.BlockSpec(memory_space=pltpu.HBM)
    return pl.pallas_call(
        element_kernel,
        in_specs=[whole, far, far, whole, whole],
        out_shape=(
            jax.ShapeDtypeStruct((pieces, samples, 3 * nodes // pieces), BF),
            jax.ShapeDtypeStruct((samples, width), F32),
        ),
        scratch_shapes=[
            pltpu.VMEM(modulus.shape, F32),
            pltpu.VMEM(connectivity.shape, jnp.int32),
            pltpu.VMEM((3 * samples, nodes + 128), BF),
            pltpu.VMEM((all_nodes, 8 * TILE), BF),
            pltpu.VMEM((3 * samples, 8 * TILE), F32),
            pltpu.VMEM((3 * samples, 8 * TILE), F32),
            pltpu.VMEM((3 * samples, all_nodes), F32),
            pltpu.SemaphoreType.DMA,
            pltpu.SemaphoreType.DMA,
        ],
        compiler_params=pltpu.CompilerParams(vmem_limit_bytes=48 << 20),
        name="elements",
    )(shared, resident(modulus), resident(connectivity), table, kron)


def fetch_leaves(source, begin, target, semaphores):
    height = target.shape[0] // len(ZIGZAG)
    width = target.shape[1]
    return [
        fetch(source.at[at * height:(at + 1) * height, begin:begin + width],
              target.at[leaf * height:(leaf + 1) * height], semaphores.at[at])
        for at, leaf in enumerate(ZIGZAG)
    ]


def resident(array):
    return pltpu.with_memory_space_constraint(array, pltpu.HBM)


def near_kernel(terms_ref, band_hbm, q_ref, part_ref, band_ref, last_ref, band_sem, last_sem):
    split = last_ref.shape[1]
    begin = band_hbm.shape[1] - split
    near, samples, width = terms_ref.shape
    band_copies = fetch_leaves(band_hbm, 0, band_ref, band_sem)
    last_copies = fetch_leaves(band_hbm, begin, last_ref, last_sem)
    half = near * width // 4
    terms = terms_ref[...].astype(F32)
    q1 = jnp.concatenate([terms[2 * k] + terms[2 * k + 1] for k in range(near // 2)], 1)
    q_ref[0] = q1
    low = q1.astype(BF)
    for copy in band_copies:
        copy.wait()
    q2 = -jnp.concatenate(
        [plain_dot(low[:, :half], band_ref[:half, :half]), plain_dot(low[:, half:], band_ref[half:2 * half, :half])], 1)
    q_ref[1] = q2
    q3 = -plain_dot(q2.astype(BF), band_ref[:, half:3 * half])
    q_ref[2] = q3
    for copy in last_copies:
        copy.wait()
    offset = 3 * half - begin
    part_ref[...] = (-plain_dot(q3.astype(BF), last_ref[:, offset:offset + 4 * half])).astype(BF)


def near_levels(terms, bands):
    near, samples, width = terms.shape
    columns = near * width // 2
    lead = -(-(3 * columns // 2) // 128) * 128
    tail = bands.shape[1] - 3 * columns // 2 // 128 * 128
    return pl.pallas_call(
        near_kernel,
        in_specs=[pl.BlockSpec(memory_space=pltpu.VMEM), pl.BlockSpec(memory_space=pltpu.HBM)],
        scratch_shapes=[
            pltpu.VMEM((columns, lead), BF),
            pltpu.VMEM((columns, tail), BF),
            pltpu.SemaphoreType.DMA((near,)),
            pltpu.SemaphoreType.DMA((near,)),
        ],
        out_shape=(
            jax.ShapeDtypeStruct((3, samples, columns), F32),
            jax.ShapeDtypeStruct((samples, 2 * columns), BF),
        ),
        compiler_params=pltpu.CompilerParams(vmem_limit_bytes=16 << 20),
        name="near_levels",
    )(terms, resident(bands))


def far_kernel(front5_ref, z4_ref, z_ref, ring_hbm, near_ref, x4_ref, x_ref, ring_ref,
               upper_sem, lower_sem):
    half = near_ref.shape[0] // 2
    height = near_ref.shape[0] // len(ZIGZAG)
    middle = ring_ref.shape[0] // 2
    upper = fetch(ring_hbm.at[:middle], ring_ref.at[:middle], upper_sem)
    lower = fetch(ring_hbm.at[middle:], ring_ref.at[middle:], lower_sem)
    upper.wait()
    first = rows_dot(front5_ref[...], ring_ref[:middle])
    lower.wait()
    x4 = z4_ref[...].astype(F32) - jnp.concatenate([first, rows_dot(front5_ref[...], ring_ref[middle:])], 1)
    x4_ref[...] = x4
    places = [ZIGZAG.index(leaf) * height for leaf in range(len(ZIGZAG))]

    def near_rows(first, last, begin, end):
        return jnp.concatenate([near_ref[at:at + height, begin:end] for at in places[first:last]], 0)

    x3 = z_ref[2].astype(F32) - rows_dot(x4.astype(BF), near_rows(0, 8, 3 * half, 7 * half))
    x_ref[2] = x3
    x2 = z_ref[1].astype(F32) - rows_dot(x3.astype(BF), near_rows(0, 8, half, 3 * half))
    x_ref[1] = x2
    low = x2.astype(BF)
    x_ref[0] = z_ref[0].astype(F32) - jnp.concatenate(
        [rows_dot(low[:, :half], near_rows(0, 4, 0, half)), rows_dot(low[:, half:], near_rows(4, 8, 0, half))], 1)


def far_levels(front5, z4, z_near, ring_band, bands):
    whole = pl.BlockSpec(memory_space=pltpu.VMEM)
    return pl.pallas_call(
        far_kernel,
        in_specs=[whole, whole, whole, pl.BlockSpec(memory_space=pltpu.HBM), whole],
        scratch_shapes=[
            pltpu.VMEM(ring_band.shape, BF),
            pltpu.SemaphoreType.DMA,
            pltpu.SemaphoreType.DMA,
        ],
        out_shape=(
            jax.ShapeDtypeStruct(z4.shape, F32),
            jax.ShapeDtypeStruct(z_near.shape, F32),
        ),
        compiler_params=pltpu.CompilerParams(vmem_limit_bytes=24 << 20),
        name="far_levels",
    )(front5, z4, z_near, resident(ring_band), bands)


def exchange(value, axis, groups=None):
    return lax.all_to_all(value, axis, 0, 0, axis_index_groups=groups, tiled=True)


def group_lists(leaves, height):
    size = 1 << height
    return [[base + i for i in range(size)] for base in range(0, leaves, size)]


def body(
    interior_disp,
    separator_disp,
    modulus,
    connectivity,
    stiffness,
    load,
    leaf_pivot_inv,
    leaf_coupling,
    pivot_inv,
    coupling,
):
    leaves = lax.axis_size("leaf")
    fronts = lax.axis_size("front")
    levels = leaves.bit_length() - 1
    leaf_index = lax.axis_index("leaf")
    samples, inner_size = interior_disp.shape
    rows = separator_disp.shape[1]
    own_samples = samples // fronts
    pairs = [(source, source ^ 1) for source in range(leaves)]
    partner = lax.ppermute(separator_disp, "leaf", pairs)
    start5 = rows * (2**5 - 4)
    partner, own_band5 = lax.optimization_barrier((partner, coupling[:, start5:2 * start5 + 4 * rows]))
    upper_leaf = leaf_index % 2 == 1
    shared = jnp.where(
        upper_leaf,
        jnp.concatenate([partner, separator_disp], 1),
        jnp.concatenate([separator_disp, partner], 1),
    )
    near = 8
    near_cols = -(-rows * (2**5 - 4) // 128) * 128
    near_groups = [[base + i for i in range(near)] for base in range(0, leaves, near)]
    ring_groups = group_lists(leaves, 4)
    spot = leaf_index % near
    zigzag_groups = [[base + at for at in ZIGZAG] for base in range(0, leaves, near)]
    near_bands = lax.all_gather(coupling[:, :near_cols], "leaf", axis_index_groups=zigzag_groups)

    def own_coupling(height):
        start = rows * (2**height - 4)
        return coupling[:, start:start + (rows << height)]

    def own_pivot(height):
        start = rows * (2**height - 2)
        return pivot_inv[:, start:start + (rows << height)]

    def joined(stack):
        return jnp.transpose(stack, (1, 0, 2)).reshape(own_samples, -1)

    def split(flat):
        return jnp.transpose(flat.reshape(own_samples, -1, rows), (1, 0, 2))

    def collect(low, height):
        sent = jnp.broadcast_to(low[None], (1 << height,) + low.shape)
        return exchange(sent, "leaf", group_lists(leaves, height))

    table, kron = prepare(interior_disp, stiffness)
    pieces, sep_terms = assemble(shared, modulus, connectivity, table, kron, fronts)
    received = exchange(pieces, "front")
    own_residual = load - jnp.sum(received.astype(F32), 0)
    own_low = own_residual.astype(BF)
    terms = -sep_terms - plain_dot(own_low, leaf_coupling)
    high = lax.reduce_precision(terms, 8, 7)
    both = jnp.concatenate([high, terms - high], 1).astype(BF).reshape(fronts, own_samples, 4 * rows)
    packed = jnp.concatenate([jnp.broadcast_to(own_low[None], (fronts,) + own_low.shape), both], 1)
    everyone = exchange(packed, "front")
    halves = jnp.sum(everyone[:, samples:].astype(F32), 0)
    term = halves[:, :2 * rows] + halves[:, 2 * rows:]
    low_residual = jnp.transpose(everyone[:, :samples], (1, 0, 2)).reshape(samples, inner_size)
    pivoted = own_residual + rows_dot(low_residual, leaf_pivot_inv)

    near_terms = exchange(jnp.broadcast_to(term.astype(BF)[None], (near,) + term.shape), "leaf", near_groups)
    bands = near_bands.reshape(near * rows, near_cols)
    near_q, part4 = near_levels(near_terms, bands)
    ring_band = lax.all_gather(
        lax.optimization_barrier((own_band5, part4))[0], "leaf",
        axis_index_groups=ring_groups,
    ).reshape(16 * rows, 32 * rows)
    q1, q2, q3 = near_q[0], near_q[1], near_q[2]
    low1, low2, low3 = q1.astype(BF), q2.astype(BF), q3.astype(BF)
    ring = 16
    across = []
    for source in range(leaves):
        place = source % ring
        other = place + (12 if place < 4 else -12 if place >= 12 else 4 if place < 8 else -4)
        across.append((source, source - place + other))
    q4 = part4.astype(F32) + lax.ppermute(part4, "leaf", across).astype(F32)
    low4 = q4.astype(BF)

    def piece(flat, index):
        return lax.dynamic_slice_in_dim(flat, index * rows, rows, 1)

    z_own = []
    for height, (value, low) in enumerate(((q1, low1), (q2, low2), (q3, low3)), 1):
        size = 1 << height
        front = lax.dynamic_slice_in_dim(low, spot // size * (size * rows), size * rows, 1)
        z_own.append(piece(value, spot) + rows_dot(front, own_pivot(height)))
    ring_spot = leaf_index % ring
    z4 = piece(q4, ring_spot) + rows_dot(low4, own_pivot(4))
    part5 = -plain_dot(piece(low4, ring_spot), own_coupling(5))
    q5 = jnp.sum(exchange(split(part5.astype(BF)), "leaf", group_lists(leaves, 5)).astype(F32), 0)
    low5 = q5.astype(BF)
    part6 = -plain_dot(low5, own_coupling(6))
    sent = jnp.concatenate(
        [split(part6.astype(BF)), jnp.broadcast_to(low5[None], (leaves,) + low5.shape)], 2)
    back = exchange(sent, "leaf")
    q6 = jnp.sum(back[:, :, :rows].astype(F32), 0)
    full5 = joined(lax.dynamic_slice_in_dim(back, leaf_index // 32 * 32, 32, 0)[:, :, rows:])
    z5 = q5 + rows_dot(full5, own_pivot(5))
    x6 = q6 + rows_dot(joined(collect(q6.astype(BF), 6)), own_pivot(6))
    x5 = z5 - rows_dot(joined(collect(x6.astype(BF), 6)), own_coupling(6))
    packed5 = jnp.concatenate([x5, z4] + z_own, 1).astype(BF)
    packed5, ring_band = lax.optimization_barrier((packed5, ring_band))
    last = collect(packed5, 5)
    same_ring = lax.dynamic_slice_in_dim(last, leaf_index % 32 // 16 * 16, 16, 0)
    nearby = lax.dynamic_slice_in_dim(last, leaf_index % 32 // near * near, near, 0)
    z_near = jnp.transpose(
        nearby[:, :, 2 * rows:].reshape(near, own_samples, 3, rows), (2, 1, 0, 3)
    ).reshape(3, own_samples, near * rows)
    x4_full, x_near = far_levels(
        joined(last[:, :, :rows]), joined(same_ring[:, :, rows:2 * rows]), z_near, ring_band, bands)
    x4 = piece(x4_full, ring_spot)
    x1, x2, x3 = x_near[0], x_near[1], x_near[2]
    corrections = [piece(x1, spot), piece(x2, spot), piece(x3, spot), x4, x5, x6]
    front_low = lax.dynamic_slice_in_dim(x1.astype(BF), spot // 2 * (2 * rows), 2 * rows, 1)
    all_samples = exchange(jnp.broadcast_to(front_low[None], (fronts,) + front_low.shape), "front")
    leaf_correction = pivoted - rows_dot(all_samples.reshape(samples, 2 * rows), leaf_coupling)
    return (leaf_correction, jnp.concatenate(corrections, 1))


def solution(mesh):
    in_specs = (
        P(None, "leaf"),
        P(None, "leaf"),
        P(None, ("leaf", "front")),
        P(None, ("leaf", "front")),
        P(),
        P(None, ("leaf", "front")),
        P(("leaf", "front"), None),
        P(("leaf", "front"), None),
        P("leaf", None),
        P("leaf", None),
    )
    out_specs = (P(None, ("leaf", "front")), P("front", "leaf"))
    return jax.shard_map(body, mesh=mesh, in_specs=in_specs, out_specs=out_specs, check_vma=False)
```
